32 devices in a mesh: dp: 4 (over y, x), seqtp: 8 (over z, core).
Axes of the slice: x: 2, y: 2, z: 4, core: 2. Of those that a mesh axis runs over, the one named last changes fastest.
Arguments:
- output_gradient: bfloat16 [2048, 4096], P(('dp', 'seqtp')), may hold values from -6 to 6
- hidden: bfloat16 [2048, 14336], P('dp', 'seqtp'), may hold values from -6 to 6
- frozen_down_weight: bfloat16 [14336, 4096], P('seqtp'), may hold values from -0.09375 to 0.09375
- adapter_input_maps: bfloat16 [24, 16, 14336], P('dp', None, 'seqtp'), may hold values from -0.1875 to 0.1875
- adapter_output_maps: bfloat16 [24, 16, 4096], P('dp', None, 'seqtp'), may hold values from -0.09375 to 0.09375
- adapter_per_block: int32 [4, 4], replicated, may hold values from 0 to 23
- live_tokens_per_block: int32 [4, 4], replicated, may hold values from 1 to 128, as said below
Outputs:
- hidden_gradient: bfloat16 [2048, 14336], P('dp', 'seqtp')
- adapter_input_gradient: float32 [24, 16, 14336], P('dp', None, 'seqtp')
- adapter_output_gradient: float32 [24, 16, 4096], P('dp', None, 'seqtp')
The draws below stay inside these ranges and needn't reach their ends.
Inputs may be any that keep to these rules, and one draw needn't show every extreme that they name: The first live_tokens_per_block tokens of a block are live, the rest padding; some block is full.
All inputs are finite; a program needn't handle non-finite values.
Results may differ from the reference program's by a relative error of at most 0.0034.
Values may be sent and summed in bfloat16 or wider, within the bound.
A program may use at most 64 MiB of HBM per device.

```python
import math
import jax
import jax.numpy as jnp
import numpy as np
from jax import lax

MODEL_FEATURES = 4096
HIDDEN_UNITS = 14336
ADAPTER_RANK = 16
BLOCK = 128
BLOCKS = 4
ADAPTER_TOTAL = 24
TOKENS = 2048
N_DP = 4


def draw_live_tokens_per_block(key, part):
    first_key, second_key = jax.random.split(key)
    filled = jax.random.randint(first_key, (N_DP * BLOCKS,), 1, BLOCK + 1, dtype=jnp.int32)
    chosen = jax.random.randint(second_key, (), 0, N_DP * BLOCKS, dtype=jnp.int32)
    filled = jnp.where(jnp.arange(N_DP * BLOCKS, dtype=jnp.int32) == chosen, BLOCK, filled)
    return filled.reshape(N_DP, BLOCKS)


def set_ends(array, rng, low, top_value):
    longest = array.shape.index(max(array.shape))
    spots = []
    for shift in (0, 1):
        where = [jax.random.randint(jax.random.fold_in(rng, axis), (), 0, length) for axis, length in enumerate(array.shape)]
        where[longest] = (where[longest] + shift) % array.shape[longest]
        spots.append(tuple(where))
    return array.at[spots[0]].set(low).at[spots[1]].set(top_value)


def block_levels(stream_key, shape, pieces, low, high):
    loudness = 1.0
    for axis_at, parts in pieces:
        steps = jax.random.uniform(jax.random.fold_in(jax.random.fold_in(stream_key, 6), axis_at), (parts,), jnp.float32, low / len(pieces), high / len(pieces))
        loudness = loudness * jnp.repeat(jnp.exp(steps), shape[axis_at] // parts).reshape((-1,) + (1,) * (len(shape) - 1 - axis_at))
    return loudness


def rank_table(count, skew):
    loads = [(1 << 20) // math.isqrt(standing ** skew) + 1 for standing in range(1, count + 1)]
    width = 1 + sum(loads) // (1 << 30)
    return np.cumsum(np.array([max(1, weight // width) for weight in loads]))


def skewed_ids(rng, shape, number_of, lean):
    table = rank_table(number_of, lean)
    pick = jax.random.randint(jax.random.fold_in(rng, 1), shape, 0, int(table[number_of - 1]))
    grade = jnp.searchsorted(jnp.asarray(table, jnp.int32), pick, side="right")
    return jax.random.permutation(jax.random.fold_in(rng, 2), number_of)[grade].astype(jnp.int32)


def gaussian(own_key, dims, spread, most, shards=(), held_as=jnp.bfloat16):
    entries = jax.random.normal(own_key, dims, jnp.float32) * spread
    if len(shards) > 0:
        entries = block_levels(own_key, dims, shards, -0.22, 0.18) * entries
    return jnp.clip(entries, min=-most, max=most).astype(held_as)


def setup_inputs(seed: int = 0) -> dict:
    key_of = jax.random.split(jax.random.key(seed), 8)
    output_gradient = gaussian(key_of[0], (TOKENS, MODEL_FEATURES), 1.0, 6.0, ((0, 32),))
    hidden = gaussian(key_of[1], (TOKENS, HIDDEN_UNITS), 1.0, 6.0, ((0, 4), (1, 8)))
    frozen_down_weight = gaussian(key_of[2], (HIDDEN_UNITS, MODEL_FEATURES), MODEL_FEATURES ** -0.5, 0.09375, ((0, 8),))
    adapter_input_maps = gaussian(key_of[3], (ADAPTER_TOTAL, ADAPTER_RANK, HIDDEN_UNITS), (HIDDEN_UNITS // 16) ** -0.5, 0.1875, ((0, 4), (2, 8)))
    adapter_output_maps = gaussian(key_of[4], (ADAPTER_TOTAL, ADAPTER_RANK, MODEL_FEATURES), MODEL_FEATURES ** -0.5, 0.09375, ((0, 4), (2, 8)))
    adapter_per_block = set_ends(skewed_ids(key_of[5], (N_DP, BLOCKS), ADAPTER_TOTAL, 2), jax.random.fold_in(key_of[5], 3), 0, ADAPTER_TOTAL - 1).astype(jnp.int32)
    live_tokens_per_block = draw_live_tokens_per_block(jax.random.fold_in(key_of[7], 71), 0)
    return {"output_gradient": output_gradient, "hidden": hidden, "frozen_down_weight": frozen_down_weight, "adapter_input_maps": adapter_input_maps, "adapter_output_maps": adapter_output_maps, "adapter_per_block": adapter_per_block, "live_tokens_per_block": live_tokens_per_block}


adapter_scale = 0.5


def reference(output_gradient, hidden, frozen_down_weight, adapter_input_maps, adapter_output_maps, adapter_per_block, live_tokens_per_block):
    group_rows = BLOCKS * BLOCK
    positions = jnp.arange(BLOCK, dtype=jnp.int32)
    adapters = jnp.arange(ADAPTER_TOTAL, dtype=jnp.int32)

    def per_group(totals, group_index):
        total_a, total_b = totals
        offset = (group_index * group_rows).astype(jnp.int32)
        grad_rows = lax.dynamic_slice_in_dim(output_gradient, offset, group_rows, 0)
        hidden_rows = lax.dynamic_slice_in_dim(hidden, offset, group_rows, 0)
        block_positions = lax.dynamic_index_in_dim(adapter_per_block, group_index, 0, keepdims=False)
        filled = lax.dynamic_index_in_dim(live_tokens_per_block, group_index, 0, keepdims=False)
        live_token_mask = (positions[None, :] < filled[:, None]).astype(jnp.float32)
        selected_input_map = jnp.take(adapter_input_maps, block_positions, axis=0).astype(jnp.float32)
        selected_output_map = jnp.take(adapter_output_maps, block_positions, axis=0).astype(jnp.float32)
        frozen_matrix = jnp.dot(grad_rows, frozen_down_weight.T, preferred_element_type=jnp.float32).reshape(BLOCKS, BLOCK, HIDDEN_UNITS)
        gradient_block_rows = grad_rows.reshape(BLOCKS, BLOCK, MODEL_FEATURES).astype(jnp.float32)
        hidden_block_rows = hidden_rows.reshape(BLOCKS, BLOCK, HIDDEN_UNITS).astype(jnp.float32)
        reduced_output = (jnp.einsum("piv,pov->poi", gradient_block_rows, selected_output_map) * live_token_mask[:, None, :]).astype(jnp.bfloat16)
        reduced_input = (jnp.einsum("bkf,brf->brk", hidden_block_rows, selected_input_map) * live_token_mask[:, None, :]).astype(jnp.bfloat16)
        reduced_output_broad = reduced_output.astype(jnp.float32)
        reduced_input_broad = reduced_input.astype(jnp.float32)
        hidden_gradient = (frozen_matrix * live_token_mask[:, :, None] + adapter_scale * jnp.einsum("acp,act->apt", reduced_output_broad, selected_input_map)).astype(jnp.bfloat16)
        per_block_input_gradient = adapter_scale * jnp.einsum("qoe,qep->qop", reduced_output_broad, hidden_block_rows)
        per_block_output_gradient = adapter_scale * jnp.einsum("xuf,xfi->xui", reduced_input_broad, gradient_block_rows)
        one_hot = (block_positions[:, None] == adapters[None, :]).astype(jnp.float32)
        group_term_a = jnp.einsum("ba,brf->arf", one_hot, per_block_input_gradient)
        group_term_b = jnp.einsum("ba,brd->ard", one_hot, per_block_output_gradient)
        totals = (total_a + group_term_a, total_b + group_term_b)
        return totals, hidden_gradient.reshape(group_rows, HIDDEN_UNITS)

    start_totals = (jnp.zeros((ADAPTER_TOTAL, ADAPTER_RANK, HIDDEN_UNITS), jnp.float32), jnp.zeros((ADAPTER_TOTAL, ADAPTER_RANK, MODEL_FEATURES), jnp.float32))
    (total_a, total_b), hidden_gradient = lax.scan(per_group, start_totals, jnp.arange(N_DP, dtype=jnp.int32))
    return hidden_gradient.reshape(N_DP * group_rows, HIDDEN_UNITS), total_a, total_b
```

```python
import functools

import jax
import jax.numpy as jnp
from jax import lax
from jax.experimental import pallas as pl
from jax.experimental.pallas import tpu as pltpu
from jax.sharding import PartitionSpec as P

adapter_scale = 0.5
MESH = pl.DeviceIdType.MESH
F32 = jnp.float32
BF16 = jnp.bfloat16


def dot_nt(a, b):
    return lax.dot_general(a, b, (((1,), (1,)), ((), ())), preferred_element_type=F32)


def dot_nn(a, b):
    return lax.dot_general(a, b, (((1,), (0,)), ((), ())), preferred_element_type=F32)


def kernel(
    nd, ntp, blocks, block, rank, held, rows, chunks, ff, feat, tiles,
    g_ref, h_ref, w_ref, a_ref, b_ref, tab, live,
    hg_ref, oa_ref, ob_ref,
    g_all, h_v, w_v, a_all, b_all, a_sel, b_sel, b_in, lo_all, lo_bf, lo_t,
    li_part, li_rs, li_all, li_bf, ga, gb, acc, hg_v, oa_v, ob_v,
    w_sem, own_sem, out_sem,
    nb_s, nb_r, sib_s, sib_r, bdp_s, bdp_r, adp_s, adp_r, bs_s, bs_r,
    lo_s, lo_r, rs_s, rs_r, li_s, li_r, ga_s, ga_r, gb_s, gb_r,
):
    nz = ntp // 2
    dp = lax.axis_index("dp")
    j = lax.axis_index("seqtp")
    z = lax.div(j, 2)
    c = lax.rem(j, 2)
    sib = z * 2 + 1 - c
    crow = rows // chunks
    tile = ff // tiles
    pair = 2 * rows
    piece = blocks * rank // ntp
    fused = pair == block

    def dp_peer(k):
        return lax.rem(dp + k, nd)

    def tp_peer(k):
        return lax.rem(j + k, ntp)

    def dp_from(k):
        return lax.rem(dp + nd - k, nd)

    def tp_from(k):
        return lax.rem(j + ntp - k, ntp)

    def slab(index, size):
        return pl.ds(pl.multiple_of(index * size, size), size)

    w_cp = lambda n: pltpu.make_async_copy(
        w_ref.at[slab(n, tile)], w_v.at[slab(n, tile)], w_sem.at[n]
    )
    own = [
        pltpu.make_async_copy(g_ref, g_all.at[slab(j, rows)], own_sem.at[0]),
        pltpu.make_async_copy(b_ref, b_all.at[pl.ds(dp * held, held)], own_sem.at[1]),
        pltpu.make_async_copy(h_ref, h_v, own_sem.at[2]),
        pltpu.make_async_copy(a_ref, a_all.at[pl.ds(dp * held, held)], own_sem.at[3]),
    ]
    own[0].start()
    own[1].start()
    for n in range(tiles):
        w_cp(n).start()
    own[2].start()
    own[3].start()

    barrier = pltpu.get_barrier_semaphore()
    for k in range(1, nd):
        pl.semaphore_signal(barrier, inc=1, device_id=(dp_peer(k), j), device_id_type=MESH)
    for k in range(1, ntp):
        pl.semaphore_signal(barrier, inc=1, device_id=(dp, tp_peer(k)), device_id_type=MESH)
    pl.semaphore_wait(barrier, nd - 1 + ntp - 1)

    def source(way, d):
        return z - d if way == 0 else z + d

    def has(way, d):
        return z >= d if way == 0 else z + d < nz

    def chunk_at(ref, first, k):
        return ref.at[pl.ds(pl.multiple_of(first + k * crow, crow), crow)]

    def nb_copy(way, d, k):
        first = (source(way, d) * 2 + c) * rows
        src = chunk_at(g_ref, 0, k) if d == 0 else chunk_at(g_all, first, k)
        return pltpu.make_async_remote_copy(
            src_ref=src, dst_ref=chunk_at(g_all, first, k),
            send_sem=nb_s.at[way, d, k], recv_sem=nb_r.at[way, d + 1, k],
            device_id=(dp, j + 2 if way == 0 else j - 2), device_id_type=MESH,
        )

    def nb_arrival(way, d, k):
        first = (source(way, d) * 2 + c) * rows
        here = chunk_at(g_all, first, k)
        return pltpu.make_async_remote_copy(
            src_ref=here, dst_ref=here,
            send_sem=nb_s.at[way, d, k], recv_sem=nb_r.at[way, d, k],
            device_id=(dp, sib), device_id_type=MESH,
        )

    def sib_copy(way, d, k, core):
        first = (source(way, d) * 2 + core) * rows
        src = chunk_at(g_ref, 0, k) if d == 0 else chunk_at(g_all, first, k)
        return pltpu.make_async_remote_copy(
            src_ref=src, dst_ref=chunk_at(g_all, first, k),
            send_sem=sib_s.at[way, d, k], recv_sem=sib_r.at[way, d, k],
            device_id=(dp, sib), device_id_type=MESH,
        )

    def send_on(way, d, k):
        @pl.when(has(way, d) & has(1 - way, 1))
        def _():
            nb_copy(way, d, k).start()

    def receive(d, k):
        for way in (0, 1):
            @pl.when(has(way, d))
            def _():
                nb_arrival(way, d, k).wait_recv()
            if d < nz - 1:
                send_on(way, d, k)

            @pl.when(has(way, d))
            def _():
                sib_copy(way, d, k, c).start()

    half = chunks // 2

    def send_own(lo, hi):
        for k in range(lo, hi):
            send_on(0, 0, k)
            send_on(1, 0, k)
            sib_copy(0, 0, k, c).start()

    send_own(0, half)

    def dp_copy(src, dst, s, r, k):
        return pltpu.make_async_remote_copy(
            src_ref=src, dst_ref=dst, send_sem=s.at[k], recv_sem=r.at[k],
            device_id=(dp_peer(k), j), device_id_type=MESH,
        )

    def tp_copy(src, dst, s, r, k):
        return pltpu.make_async_remote_copy(
            src_ref=src, dst_ref=dst, send_sem=s.at[k], recv_sem=r.at[k],
            device_id=(dp, tp_peer(k)), device_id_type=MESH,
        )

    def b_copy(k, who):
        return dp_copy(b_ref, b_all.at[pl.ds(who * held, held)], bdp_s, bdp_r, k)

    def a_copy(k, who):
        return dp_copy(a_ref, a_all.at[pl.ds(who * held, held)], adp_s, adp_r, k)

    for k in range(1, nd):
        b_copy(k, dp).start()
    for k in range(1, nd):
        a_copy(k, dp).start()

    def block_of(index):
        return lax.div(index * rows, block)

    own[1].wait()
    for k in range(1, nd):
        b_copy(k, dp_from(k)).wait_recv()
    for b in range(blocks):
        b_sel[b] = b_all[tab[dp, b]]
    b_in[j] = b_sel[block_of(j)]

    def bs_copy(k, who, whose):
        return tp_copy(b_sel.at[block_of(whose)], b_in.at[who], bs_s, bs_r, k)

    for k in range(1, ntp):
        bs_copy(k, j, tp_peer(k)).start()
    send_own(half, chunks)

    own[0].wait()
    for k in range(chunks):
        sib_copy(0, 0, k, 1 - c).wait_recv()

    def product(first, size, n):
        return dot_nt(g_all[pl.ds(first, size), :], w_v[slab(n, tile), :])

    def finish(zb, b, n, value):
        cols = slab(n, tile) if tiles > 1 else pl.ds(0, tile)
        filled = live[dp, b]
        keep = (lax.broadcasted_iota(jnp.int32, (block, 1), 0) < filled).astype(F32)
        extra = dot_nn(lo_t[b], a_sel[b, :, cols])
        hg_v[slab(b, block), cols] = (value * keep + adapter_scale * extra).astype(BF16)

    def mm_tiles(zb, lo, hi, final, wait_w):
        def one(n, carry):
            if wait_w:
                w_cp(n).wait()
            first = pl.multiple_of(zb * pair, pair)
            value = product(first, pair, n)
            if final:
                finish(zb, zb, n, value)
            else:
                cols = slab(n, tile) if tiles > 1 else pl.ds(0, tile)
                acc[pl.ds(first, pair), cols] = value
            return carry
        lax.fori_loop(lo, hi, one, 0)

    def fin_tiles(b):
        def one(n, carry):
            cols = slab(n, tile) if tiles > 1 else pl.ds(0, tile)
            finish(b, b, n, acc[slab(b, block), cols])
            return carry
        lax.fori_loop(0, tiles, one, 0)

    def hg_out(zb):
        return pltpu.make_async_copy(
            hg_v.at[slab(zb, block)], hg_ref.at[slab(zb, block)], out_sem.at[2 + zb]
        )

    def step(d, final, start=0, stop=chunks):
        def one(k, carry):
            if d + 1 < nz:
                receive(d + 1, k)
            lo, hi = lax.div(tiles * k, chunks), lax.div(tiles * (k + 1), chunks)
            for way in (0, 1) if d else (0,):
                @pl.when(has(way, d))
                def _():
                    mm_tiles(source(way, d), lo, hi, final, d == 0)
            return carry
        if start < stop:
            lax.fori_loop(start, stop, one, 0)
        if final and stop == chunks:
            for way in (0, 1) if d else (0,):
                @pl.when(has(way, d))
                def _():
                    hg_out(source(way, d)).start()

    def siblings(d):
        for way in (0, 1):
            @pl.when(has(way, d))
            def _():
                for k in range(chunks):
                    sib_copy(way, d, k, 1 - c).wait_recv()

    step(0, False, 0, half)

    for k in range(1, ntp):
        bs_copy(k, tp_from(k), j).wait_recv()
    low = jnp.zeros((rank, rows), F32)
    for s in range(ntp):
        low = low + dot_nt(b_in[s], g_all[slab(j, rows), s * feat : (s + 1) * feat])
    offset = lax.rem(j * rows, block)
    live_here = lax.broadcasted_iota(jnp.int32, (rank, rows), 1) + offset < live[dp, block_of(j)]
    low = (low * live_here.astype(F32)).astype(BF16)
    place = (
        lax.broadcasted_iota(jnp.int32, (rows, block), 1)
        == lax.broadcasted_iota(jnp.int32, (rows, block), 0) + offset
    ).astype(F32).astype(BF16)
    lo_all[j] = dot_nn(low, place).astype(BF16)

    def lo_copy(k, who):
        return tp_copy(lo_all.at[who], lo_all.at[who], lo_s, lo_r, k)

    for k in range(1, ntp):
        lo_copy(k, j).start()

    step(0, False, half)

    own[2].wait()
    for k in range(1, ntp):
        lo_copy(k, tp_from(k)).wait_recv()
    per_block = block // rows
    for b in range(blocks):
        value = lo_all[b * per_block].astype(F32)
        for s in range(1, per_block):
            value = value + lo_all[b * per_block + s].astype(F32)
        lo_bf[b] = value.astype(BF16)
        lo_t[b] = value.T.astype(BF16)
        ga[dp, b * rank : (b + 1) * rank, :] = (
            adapter_scale * dot_nn(lo_bf[b], h_v[b * block : (b + 1) * block, :])
        ).astype(BF16)

    def ga_copy(k, who):
        return dp_copy(ga.at[who], ga.at[who], ga_s, ga_r, k)

    def gb_copy(k, who):
        return dp_copy(gb.at[who], gb.at[who], gb_s, gb_r, k)

    for k in range(1, nd):
        ga_copy(k, dp).start()

    siblings(1)
    step(1, False, 0, half)

    own[3].wait()
    for k in range(1, nd):
        a_copy(k, dp_from(k)).wait_recv()
    for b in range(blocks):
        a_sel[b] = a_all[tab[dp, b]]
        value = dot_nt(a_sel[b], h_v[b * block : (b + 1) * block, :])
        for i in range(rank // piece):
            li_part[b * (rank // piece) + i] = value[i * piece : (i + 1) * piece, :]
    li_rs[j] = li_part[j]

    def rs_copy(k, who, whose):
        return tp_copy(li_part.at[whose], li_rs.at[who], rs_s, rs_r, k)

    for k in range(1, ntp):
        rs_copy(k, j, tp_peer(k)).start()

    step(1, False, half)

    for k in range(1, ntp):
        rs_copy(k, tp_from(k), j).wait_recv()
    total = li_rs[0]
    for s in range(1, ntp):
        total = total + li_rs[s]
    li_all[j] = total

    def li_copy(k, who):
        return tp_copy(li_all.at[who], li_all.at[who], li_s, li_r, k)

    for k in range(1, ntp):
        li_copy(k, j).start()

    if fused:
        for d in (0, 1):
            for way in (0, 1) if d else (0,):
                @pl.when(has(way, d))
                def _():
                    fin_tiles(source(way, d))
                    hg_out(source(way, d)).start()

    siblings(2)
    step(2, fused, 0, half)

    for k in range(1, ntp):
        li_copy(k, tp_from(k)).wait_recv()
    group = rank // piece
    for b in range(blocks):
        value = jnp.concatenate([li_all[b * group + i] for i in range(group)], axis=0)
        keep = lax.broadcasted_iota(jnp.int32, (rank, block), 1) < live[dp, b]
        li_bf[b] = (value * keep.astype(F32)).astype(BF16)

    def gb_block(b):
        gb[dp, slab(b, rank), :] = (
            adapter_scale * dot_nn(li_bf[b], g_all[slab(b, block), slab(j, feat)])
        ).astype(BF16)

    def gb_blocks(d):
        for way in (0, 1) if d else (0,):
            @pl.when(has(way, d))
            def _():
                gb_block(source(way, d))

    if fused:
        for d in range(nz - 1):
            gb_blocks(d)

    def chooser(g):
        r = lax.broadcasted_iota(jnp.int32, (held * rank, blocks * rank), 0)
        q = lax.broadcasted_iota(jnp.int32, (held * rank, blocks * rank), 1)
        same = (r & (rank - 1)) == (q & (rank - 1))
        which = jnp.zeros_like(q)
        for b in range(blocks):
            lane = (q >= b * rank) & (q < (b + 1) * rank)
            which = jnp.where(lane, tab[g, b] - dp * held, which)
        hit = (r >= which * rank) & (r < (which + 1) * rank) & same
        return hit.astype(F32).astype(BF16)

    picks = [chooser(g) for g in range(nd)]
    for k in range(1, nd):
        ga_copy(k, dp_from(k)).wait_recv()
    total = dot_nn(picks[0], ga[0])
    for g in range(1, nd):
        total = total + dot_nn(picks[g], ga[g])
    oa_v[...] = total.reshape(held, rank, ff)
    oa_cp = pltpu.make_async_copy(oa_v, oa_ref, out_sem.at[0])
    oa_cp.start()
    step(2, fused, half)
    for d in range(3, nz - 1):
        siblings(d)
        step(d, fused)

    siblings(nz - 1)
    if fused:
        gb_blocks(nz - 1)
    else:
        for b in range(blocks):
            gb_block(b)
    for k in range(1, nd):
        gb_copy(k, dp).start()

    step(nz - 1, fused)
    if not fused:
        for b in range(blocks):
            fin_tiles(b)
            hg_out(b).start()

    for k in range(1, nd):
        gb_copy(k, dp_from(k)).wait_recv()
    total = dot_nn(picks[0], gb[0])
    for g in range(1, nd):
        total = total + dot_nn(picks[g], gb[g])
    ob_v[...] = total.reshape(held, rank, feat)
    ob_cp = pltpu.make_async_copy(ob_v, ob_ref, out_sem.at[1])
    ob_cp.start()

    for d in range(nz):
        for way in (0, 1):
            if d < nz - 1:
                @pl.when(has(way, d) & has(1 - way, 1))
                def _():
                    for k in range(chunks):
                        nb_copy(way, d, k).wait_send()
            if d or way == 0:
                @pl.when(has(way, d))
                def _():
                    for k in range(chunks):
                        sib_copy(way, d, k, c).wait_send()
    for k in range(1, nd):
        for copy in (b_copy, a_copy, ga_copy, gb_copy):
            copy(k, dp).wait_send()
    for k in range(1, ntp):
        bs_copy(k, j, tp_peer(k)).wait_send()
        rs_copy(k, j, tp_peer(k)).wait_send()
        lo_copy(k, j).wait_send()
        li_copy(k, j).wait_send()
    for b in range(blocks):
        hg_out(b).wait()
    oa_cp.wait()
    ob_cp.wait()


def copy_kernel(blocks, hg, oa, ob, hg_out, oa_out, ob_out, hg_v, oa_v, ob_v, in_sem, out_sem):
    size = hg.shape[0] // blocks
    stages = [
        tuple(ref.at[pl.ds(b * size, size)] for ref in (hg, hg_v, hg_out)) for b in range(blocks)
    ] + [(oa, oa_v, oa_out), (ob, ob_v, ob_out)]
    loads = [pltpu.make_async_copy(s, v, in_sem.at[i]) for i, (s, v, _) in enumerate(stages)]
    stores = [pltpu.make_async_copy(v, o, out_sem.at[i]) for i, (_, v, o) in enumerate(stages)]
    for load in loads:
        load.start()
    for load, store in zip(loads, stores):
        load.wait()
        store.start()
    for store in stores:
        store.wait()


def shards(nd, ntp, g, h, w, a, bm, tab, live):
    blocks = tab.shape[1]
    group_rows, ff = h.shape
    block = group_rows // blocks
    held, rank, _ = a.shape
    feat = bm.shape[2]
    rows, width = g.shape
    nz = ntp // 2
    chunks = max(1, min(2, rows // 16))
    tiles = ff // 256 if ff % 256 == 0 else 1
    piece = blocks * rank // ntp
    V = pltpu.VMEM
    dma = lambda *s: pltpu.SemaphoreType.DMA(s)
    scratch = [
        V((group_rows, width), BF16), V((group_rows, ff), BF16), V((ff, width), BF16),
        V((nd * held, rank, ff), BF16), V((nd * held, rank, feat), BF16),
        V((blocks, rank, ff), BF16), V((blocks, rank, feat), BF16),
        V((ntp, rank, feat), BF16), V((ntp, rank, block), BF16),
        V((blocks, rank, block), BF16), V((blocks, block, rank), BF16),
        V((ntp, piece, block), F32), V((ntp, piece, block), F32), V((ntp, piece, block), F32),
        V((blocks, rank, block), BF16),
        V((nd, blocks * rank, ff), BF16), V((nd, blocks * rank, feat), BF16),
        V((group_rows, ff), F32), V((group_rows, ff), BF16),
        V((held, rank, ff), F32), V((held, rank, feat), F32),
        dma(tiles), dma(4), dma(2 + blocks),
        dma(2, nz, chunks), dma(2, nz + 1, chunks), dma(2, nz, chunks), dma(2, nz, chunks),
        dma(nd), dma(nd), dma(nd), dma(nd), dma(ntp), dma(ntp),
        dma(ntp), dma(ntp), dma(ntp), dma(ntp), dma(ntp), dma(ntp),
        dma(nd), dma(nd), dma(nd), dma(nd),
    ]
    any_spec = pl.BlockSpec(memory_space=pl.ANY)
    smem = pl.BlockSpec(memory_space=pltpu.SMEM)
    hg, oa, ob = pl.pallas_call(
        functools.partial(
            kernel, nd, ntp, blocks, block, rank, held, rows, chunks, ff, feat, tiles
        ),
        out_shape=(
            jax.ShapeDtypeStruct((group_rows, ff), BF16),
            jax.ShapeDtypeStruct((held, rank, ff), F32),
            jax.ShapeDtypeStruct((held, rank, feat), F32),
        ),
        in_specs=[any_spec] * 5 + [smem] * 2,
        out_specs=(any_spec,) * 3,
        scratch_shapes=scratch,
        compiler_params=pltpu.CompilerParams(
            collective_id=0, has_side_effects=True, vmem_limit_bytes=62 * 1024 * 1024
        ),
    )(g, h, w, a, bm, tab, live)
    results = (hg, oa, ob)
    return pl.pallas_call(
        functools.partial(copy_kernel, blocks),
        out_shape=tuple(jax.ShapeDtypeStruct(x.shape, x.dtype) for x in results),
        in_specs=[any_spec] * 3,
        out_specs=(any_spec,) * 3,
        scratch_shapes=[V(x.shape, x.dtype) for x in results] + [dma(blocks + 2), dma(blocks + 2)],
        compiler_params=pltpu.CompilerParams(vmem_limit_bytes=62 * 1024 * 1024),
    )(*results)


def line_kernel(
    nd, nz, blocks, block, rank, held, rows, sizes, ff, feat, width,
    g_ref, h_ref, w_ref, a_ref, b_ref, tab, live,
    hg_v, oa_v, ob_v,
    g_all, h_v, w_v, a_all, b_all, a_sel, b_sel, b_in, lo_part, lo_all, lo_t,
    li_part, li_sib, li_sum, li_rs, li_all, ga, gb, acc,
    w_sem, own_sem, relay,
    nb_s, nb_r, sib_s, sib_r, row_s, row_r, bdp_s, bdp_r, adp_s, adp_r,
    bs_s, bs_r, lo_s, lo_r, rs_s, rs_r, ag_s, ag_r, pair_s, pair_r,
    ga_s, ga_r, gb_s, gb_r,
):
    dp = lax.axis_index("dp")
    j = lax.axis_index("seqtp")
    z = lax.div(j, 2)
    c = lax.rem(j, 2)
    sib = z * 2 + 1 - c
    chunks = len(sizes)
    tile = 256
    tiles = ff // tile
    piece = blocks * rank // (2 * nz)
    pair_rows = 2 * block
    near = lax.div(z, 2)
    far = 1 - near
    starts = [sum(sizes[:i]) for i in range(chunks)]

    def slab(index, size):
        return pl.ds(pl.multiple_of(index * size, size), size)

    def has(way, d):
        return z >= d if way == 0 else z + d < nz

    def source(way, d):
        return z - d if way == 0 else z + d

    def dp_peer(k):
        return lax.rem(dp + k, nd)

    def dp_from(k):
        return lax.rem(dp + nd - k, nd)

    def z_peer(k):
        return lax.rem(z + k, nz)

    def z_from(k):
        return lax.rem(z + nz - k, nz)

    def toward(way):
        return (dp, j + 2 if way == 0 else j - 2)

    barrier = pltpu.get_barrier_semaphore()
    for way in (0, 1):
        @pl.when(has(1 - way, 1))
        def _():
            pl.semaphore_signal(barrier, inc=1, device_id=toward(way), device_id_type=MESH)
    pl.semaphore_signal(barrier, inc=1, device_id=(dp, sib), device_id_type=MESH)
    for k in range(1, nd):
        pl.semaphore_signal(barrier, inc=1, device_id=(dp_peer(k), j), device_id_type=MESH)

    own = [
        pltpu.make_async_copy(b_ref, b_all.at[pl.ds(dp * held, held)], own_sem.at[0]),
        pltpu.make_async_copy(g_ref, g_all.at[slab(j, rows)], own_sem.at[1]),
        pltpu.make_async_copy(h_ref, h_v, own_sem.at[2]),
        pltpu.make_async_copy(a_ref, a_all.at[pl.ds(dp * held, held)], own_sem.at[3]),
    ]
    w_cp = [
        pltpu.make_async_copy(w_ref.at[pl.ds(n * tile, tile)], w_v.at[pl.ds(n * tile, tile)], w_sem.at[n])
        for n in range(tiles)
    ]
    own[0].start()
    own[1].start()

    @pl.when(has(0, 1) & has(1, 1))
    def _():
        pl.semaphore_wait(barrier, nd + 2)

    @pl.when(jnp.logical_not(has(0, 1) & has(1, 1)))
    def _():
        pl.semaphore_wait(barrier, nd + 1)

    def part(ref, first, way, i):
        start = starts[i] if way == 1 else width - starts[i] - sizes[i]
        return ref.at[slab(first, rows), pl.ds(start, sizes[i])]

    def nb_copy(way, d, i):
        first = source(way, d) * 2 + c
        src = part(g_ref, 0, way, i) if d == 0 else part(g_all, first, way, i)
        return pltpu.make_async_remote_copy(
            src_ref=src, dst_ref=part(g_all, first, way, i),
            send_sem=nb_s.at[way, d, i], recv_sem=nb_r.at[way, d + 1, i],
            device_id=toward(way), device_id_type=MESH,
        )

    def nb_arrival(way, d, i):
        here = part(g_all, source(way, d) * 2 + c, way, i)
        return pltpu.make_async_remote_copy(
            src_ref=here, dst_ref=here,
            send_sem=nb_s.at[way, d - 1, i], recv_sem=nb_r.at[way, d, i],
            device_id=(dp, sib), device_id_type=MESH,
        )

    def sib_copy(way, d, i, core):
        here = part(g_all, source(way, d) * 2 + core, way, i)
        return pltpu.make_async_remote_copy(
            src_ref=here, dst_ref=here,
            send_sem=sib_s.at[way, d, i], recv_sem=sib_r.at[way, d, i],
            device_id=(dp, sib), device_id_type=MESH,
        )

    def row_copy(index):
        return pltpu.make_async_remote_copy(
            src_ref=g_ref, dst_ref=g_all.at[slab(index, rows)],
            send_sem=row_s, recv_sem=row_r, device_id=(dp, sib), device_id_type=MESH,
        )

    def send_own(lo, hi):
        for i in range(lo, hi):
            for way in (0, 1):
                @pl.when(has(1 - way, 1))
                def _():
                    nb_copy(way, 0, i).start()

    def event(n):
        d, i = n // chunks + 1, n % chunks
        for way in (0, 1):
            @pl.when(has(way, d))
            def _():
                nb_arrival(way, d, i).wait_recv()
                if d < nz - 1:
                    @pl.when(has(1 - way, 1))
                    def _():
                        nb_copy(way, d, i).start()
                sib_copy(way, d, i, c).start()

    def landed(n):
        d, i = n // chunks + 1, n % chunks
        for way in (0, 1):
            @pl.when(has(way, d))
            def _():
                sib_copy(way, d, i, 1 - c).wait_recv()

    def dp_copy(src, dst, s, r, k):
        return pltpu.make_async_remote_copy(
            src_ref=src, dst_ref=dst, send_sem=s.at[k], recv_sem=r.at[k],
            device_id=(dp_peer(k), j), device_id_type=MESH,
        )

    def z_copy(src, dst, s, r, k):
        return pltpu.make_async_remote_copy(
            src_ref=src, dst_ref=dst, send_sem=s.at[k], recv_sem=r.at[k],
            device_id=(dp, z_peer(k) * 2 + c), device_id_type=MESH,
        )

    def core_copy(src, dst, k):
        return pltpu.make_async_remote_copy(
            src_ref=src, dst_ref=dst, send_sem=pair_s.at[k], recv_sem=pair_r.at[k],
            device_id=(dp, sib), device_id_type=MESH,
        )

    def b_copy(k, who):
        return dp_copy(b_ref, b_all.at[pl.ds(who * held, held)], bdp_s, bdp_r, k)

    def a_copy(k, who):
        return dp_copy(a_ref, a_all.at[pl.ds(who * held, held)], adp_s, adp_r, k)

    def bs_copy(k, who, whose):
        return z_copy(b_sel.at[whose], b_in.at[who], bs_s, bs_r, k)

    def lo_copy(k, who):
        return z_copy(lo_all.at[who], lo_all.at[who], lo_s, lo_r, k)

    def rs_copy(k, who, whose):
        return z_copy(li_sum.at[whose], li_rs.at[who], rs_s, rs_r, k)

    def ag_copy(k, who):
        return z_copy(li_all.at[c * nz + who], li_all.at[c * nz + who], ag_s, ag_r, k)

    def ga_copy(k, who):
        return dp_copy(ga.at[who], ga.at[who], ga_s, ga_r, k)

    def gb_copy(k, who):
        return dp_copy(gb.at[who], gb.at[who], gb_s, gb_r, k)

    def lo_pair(core):
        return core_copy(lo_part.at[core], lo_part.at[core], 0)

    def li_pair(core):
        return core_copy(li_part.at[1 - core], li_sib, 1)

    def ag_pair(core):
        here = li_all.at[pl.ds(core * nz, nz)]
        return core_copy(here, here, 2)

    half = chunks // 2
    send_own(0, half)
    for k in range(1, nd):
        b_copy(k, dp).start()
    row_copy(j).start()
    for way in (0, 1):
        @pl.when(has(way, 1) & has(1 - way, 1))
        def _():
            pl.semaphore_signal(relay.at[way, 2], inc=1, device_id=toward(way), device_id_type=MESH)
    for n in range(tiles):
        w_cp[n].start()
    own[2].start()
    own[3].start()
    for k in range(1, nd):
        a_copy(k, dp).start()
    send_own(half, chunks)

    for d in range(2, nz):
        for way in (0, 1):
            @pl.when(has(way, d))
            def _():
                pl.semaphore_wait(relay.at[way, d], 1)
                if d + 1 < nz:
                    @pl.when(has(1 - way, 1))
                    def _():
                        pl.semaphore_signal(
                            relay.at[way, d + 1], inc=1, device_id=toward(way), device_id_type=MESH
                        )

    own[0].wait()
    for k in range(1, nd):
        b_copy(k, dp_from(k)).wait_recv()
    for b in range(blocks):
        b_sel[b] = b_all[tab[dp, b]]
    b_in[z] = b_sel[z]
    for k in range(1, nz):
        bs_copy(k, z, z_peer(k)).start()

    event(0)

    own[1].wait()
    row_copy(sib).wait_recv()
    for k in range(1, nz):
        bs_copy(k, z_from(k), z).wait_recv()
    low = jnp.zeros((rank, block), F32)
    for s in range(nz):
        low = low + dot_nt(b_in[s], g_all[slab(z, block), slab(2 * s + c, feat)])
    lo_part[c] = low
    lo_pair(c).start()

    event(1)

    lo_pair(1 - c).wait_recv()
    lanes = lax.broadcasted_iota(jnp.int32, (rank, block), 1)
    low = lo_part[0] + lo_part[1]
    lo_all[z] = (low * (lanes < live[dp, z]).astype(F32)).astype(BF16)
    for k in range(1, nz):
        lo_copy(k, z).start()

    event(2)

    own[3].wait()
    for k in range(1, nd):
        a_copy(k, dp_from(k)).wait_recv()
    own[2].wait()
    for b in range(blocks):
        a_sel[b] = a_all[tab[dp, b]]
        value = dot_nt(a_sel[b], h_v[b * block : (b + 1) * block, :])
        for i in range(rank // piece):
            at = b * (rank // piece) + i
            li_part[at // nz, at % nz] = value[i * piece : (i + 1) * piece, :]
    li_pair(c).start()
    for k in range(1, nz):
        lo_copy(k, z_from(k)).wait_recv()
    for b in range(blocks):
        lo_t[b] = lo_all[b].astype(F32).T.astype(BF16)
        ga[dp, b * rank : (b + 1) * rank, :] = (
            adapter_scale * dot_nn(lo_all[b], h_v[b * block : (b + 1) * block, :])
        ).astype(BF16)
    for k in range(1, nd):
        ga_copy(k, dp).start()

    event(3)

    li_pair(1 - c).wait_recv()
    li_sum[...] = li_part[c] + li_sib[...]
    li_rs[z] = li_sum[z]
    for k in range(1, nz):
        rs_copy(k, z, z_peer(k)).start()

    def keep_of(b):
        return (lax.broadcasted_iota(jnp.int32, (block, 1), 0) < live[dp, b]).astype(F32)

    for n in range(chunks):
        landed(n)
    for n in range(tiles):
        w_cp[n].wait()

    def near_tiles(lo, hi):
        def one(n, carry):
            cols = slab(n, tile)
            value = dot_nt(g_all[slab(near, pair_rows), :], w_v[slab(n, tile), :])
            for s in range(2):
                b = near * 2 + s
                extra = dot_nn(lo_t[b], a_sel[b, :, cols])
                total = value[s * block : (s + 1) * block] + adapter_scale * extra
                hg_v[slab(b, block), cols] = (total * keep_of(b)).astype(BF16)
            return carry
        lax.fori_loop(lo, hi, one, 0)

    near_tiles(0, tiles // 3)
    event(chunks)

    for k in range(1, nz):
        rs_copy(k, z_from(k), z).wait_recv()
    total = li_rs[0]
    for s in range(1, nz):
        total = total + li_rs[s]
    whole = c * nz + z
    lanes = lax.broadcasted_iota(jnp.int32, (piece, block), 1)
    filled = live[dp, lax.div(whole * piece, rank)]
    li_all[whole] = (total * (lanes < filled).astype(F32)).astype(BF16)
    for k in range(1, nz):
        ag_copy(k, z).start()

    near_tiles(tiles // 3, 2 * tiles // 3)
    event(chunks + 1)
    for k in range(1, nz):
        ag_copy(k, z_from(k)).wait_recv()
    ag_pair(c).start()
    near_tiles(2 * tiles // 3, tiles)
    event(chunks + 2)

    ag_pair(1 - c).wait_recv()

    def gb_block(b):
        group = rank // piece
        rows_of = jnp.concatenate(
            [li_all[b * group + i].astype(F32) for i in range(group)], axis=0
        ).astype(BF16)
        gb[dp, slab(b, rank), :] = (
            adapter_scale * dot_nn(rows_of, g_all[slab(b, block), slab(j, feat)])
        ).astype(BF16)

    for s in range(2):
        gb_block(near * 2 + s)

    def chooser(g):
        r = lax.broadcasted_iota(jnp.int32, (held * rank, blocks * rank), 0)
        q = lax.broadcasted_iota(jnp.int32, (held * rank, blocks * rank), 1)
        same = (r & (rank - 1)) == (q & (rank - 1))
        which = jnp.zeros_like(q)
        for b in range(blocks):
            lane = (q >= b * rank) & (q < (b + 1) * rank)
            which = jnp.where(lane, tab[g, b] - dp * held, which)
        hit = (r >= which * rank) & (r < (which + 1) * rank) & same
        return hit.astype(F32).astype(BF16)

    def owned(ref):
        total = dot_nn(chooser(0), ref[0])
        for g in range(1, nd):
            total = total + dot_nn(chooser(g), ref[g])
        return total

    for k in range(1, nd):
        ga_copy(k, dp_from(k)).wait_recv()
    oa_v[...] = owned(ga).reshape(held, rank, ff)

    for n in range(chunks + 3, 2 * chunks):
        event(n)
    for s in range(2):
        b = far * 2 + s
        acc[s * block : (s + 1) * block, :] = adapter_scale * dot_nn(lo_t[b], a_sel[b])

    def drain(d):
        for way in (0, 1):
            for i in range(chunks):
                if d < nz - 1:
                    @pl.when(has(way, d) & has(1 - way, 1))
                    def _():
                        nb_copy(way, d, i).wait_send()
                if d:
                    @pl.when(has(way, d))
                    def _():
                        sib_copy(way, d, i, c).wait_send()

    row_copy(j).wait_send()
    drain(0)
    drain(1)
    for k in range(1, nd):
        for copy in (b_copy, a_copy, ga_copy):
            copy(k, dp).wait_send()
    for k in range(1, nz):
        bs_copy(k, z, z_peer(k)).wait_send()
        lo_copy(k, z).wait_send()
        rs_copy(k, z, z_peer(k)).wait_send()
        ag_copy(k, z).wait_send()
    for copy in (lo_pair, li_pair, ag_pair):
        copy(c).wait_send()
    for n in range(chunks, 2 * chunks):
        landed(n)

    def far_chunk(i, last):
        start = jnp.where(z < nz // 2, starts[i], width - starts[i] - sizes[i])
        deep = pl.ds(pl.multiple_of(start, 128), sizes[i])
        keep = jnp.concatenate([keep_of(far * 2 + s) for s in range(2)], axis=0) if last else None
        rows_at = slab(far, pair_rows)
        for n in range(tiles):
            cols = pl.ds(n * tile, tile)
            value = acc[:, cols] + dot_nt(g_all[rows_at, deep], w_v[cols, deep])
            if last:
                hg_v[rows_at, cols] = (value * keep).astype(BF16)
            else:
                acc[:, cols] = value

    for i in range(chunks):
        event(2 * chunks + i)
        landed(2 * chunks + i)
        far_chunk(i, i == chunks - 1)
        if i == 0:
            for s in range(2):
                gb_block(far * 2 + s)
            for k in range(1, nd):
                gb_copy(k, dp).start()
        if i == chunks - 2:
            for k in range(1, nd):
                gb_copy(k, dp_from(k)).wait_recv()
            ob_v[...] = owned(gb).reshape(held, rank, feat)
            for k in range(1, nd):
                gb_copy(k, dp).wait_send()
            drain(2)
    for d in range(3, nz):
        drain(d)


def store_kernel(blocks, hg, oa, ob, hg_out, oa_out, ob_out, sem):
    size = hg.shape[0] // blocks
    copies = [
        (hg.at[pl.ds(b * size, size)], hg_out.at[pl.ds(b * size, size)]) for b in range(blocks)
    ] + [(oa, oa_out), (ob, ob_out)]
    copies = [pltpu.make_async_copy(s, o, sem.at[i]) for i, (s, o) in enumerate(copies)]
    for copy in copies:
        copy.start()
    for copy in copies:
        copy.wait()


def line_shards(nd, ntp, g, h, w, a, bm, tab, live):
    blocks = tab.shape[1]
    group_rows, ff = h.shape
    block = group_rows // blocks
    held, rank, _ = a.shape
    feat = bm.shape[2]
    rows, width = g.shape
    nz = ntp // 2
    sizes = (width // 4,) * 4
    tiles = ff // 256
    chunks = len(sizes)
    piece = blocks * rank // ntp
    V = pltpu.VMEM
    dma = lambda *s: pltpu.SemaphoreType.DMA(s)
    scratch = [
        V((group_rows, width), BF16), V((group_rows, ff), BF16), V((ff, width), BF16),
        V((nd * held, rank, ff), BF16), V((nd * held, rank, feat), BF16),
        V((blocks, rank, ff), BF16), V((blocks, rank, feat), BF16), V((nz, rank, feat), BF16),
        V((2, rank, block), F32), V((blocks, rank, block), BF16), V((blocks, block, rank), BF16),
        V((2, nz, piece, block), F32), V((nz, piece, block), F32), V((nz, piece, block), F32),
        V((nz, piece, block), F32), V((ntp, piece, block), BF16),
        V((nd, blocks * rank, ff), BF16), V((nd, blocks * rank, feat), BF16),
        V((2 * block, ff), F32),
        dma(tiles), dma(4), pltpu.SemaphoreType.REGULAR((2, nz)),
        dma(2, nz, chunks), dma(2, nz + 1, chunks), dma(2, nz, chunks), dma(2, nz, chunks),
        pltpu.SemaphoreType.DMA, pltpu.SemaphoreType.DMA,
        dma(nd), dma(nd), dma(nd), dma(nd),
        dma(nz), dma(nz), dma(nz), dma(nz), dma(nz), dma(nz), dma(nz), dma(nz), dma(3), dma(3),
        dma(nd), dma(nd), dma(nd), dma(nd),
    ]
    hbm = pl.BlockSpec(memory_space=pltpu.HBM)
    smem = pl.BlockSpec(memory_space=pltpu.SMEM)
    vmem = pl.BlockSpec(memory_space=pltpu.VMEM)
    results = pl.pallas_call(
        functools.partial(
            line_kernel, nd, nz, blocks, block, rank, held, rows, sizes, ff, feat, width
        ),
        out_shape=(
            V((group_rows, ff), BF16), V((held, rank, ff), F32), V((held, rank, feat), F32),
        ),
        in_specs=[hbm] * 5 + [smem] * 2,
        out_specs=(vmem,) * 3,
        scratch_shapes=scratch,
        compiler_params=pltpu.CompilerParams(
            collective_id=1, has_side_effects=True, vmem_limit_bytes=61 * 1024 * 1024
        ),
    )(g, h, w, a, bm, tab, live)
    return pl.pallas_call(
        functools.partial(store_kernel, blocks),
        out_shape=tuple(jax.ShapeDtypeStruct(x.shape, x.dtype) for x in results),
        in_specs=[vmem] * 3,
        out_specs=(hbm,) * 3,
        scratch_shapes=[dma(blocks + 2)],
        compiler_params=pltpu.CompilerParams(vmem_limit_bytes=8 * 1024 * 1024),
    )(*results)


def body(nd, ntp, g, h, w, a, bm, tab, live):
    blocks = tab.shape[1]
    group_rows, ff = h.shape
    rows, width = g.shape
    line = (
        ntp == 8 and blocks == 4 and 8 * rows == group_rows and ff % 256 == 0
        and width == ntp * bm.shape[2] and bm.shape[2] % 128 == 0
        and blocks * a.shape[1] == 8 * ntp
    )
    return (line_shards if line else shards)(nd, ntp, g, h, w, a, bm, tab, live)


def solution(mesh):
    in_specs = (
        P(("dp", "seqtp"), None),
        P("dp", "seqtp"),
        P("seqtp", None),
        P("dp", None, "seqtp"),
        P("dp", None, "seqtp"),
        P(),
        P(),
    )
    out_specs = (P("dp", "seqtp"), P("dp", None, "seqtp"), P("dp", None, "seqtp"))
    step = functools.partial(body, mesh.shape["dp"], mesh.shape["seqtp"])
    return jax.shard_map(step, mesh=mesh, in_specs=in_specs, out_specs=out_specs, check_vma=False)
```

```python
import functools

import jax
import jax.numpy as jnp
from jax import lax
from jax.experimental import pallas as pl
from jax.experimental.pallas import tpu as pltpu
from jax.sharding import PartitionSpec as P

adapter_scale = 0.5
MESH = pl.DeviceIdType.MESH
F32 = jnp.float32
BF16 = jnp.bfloat16


def dot_nt(a, b):
    return lax.dot_general(a, b, (((1,), (1,)), ((), ())), preferred_element_type=F32)


def dot_nn(a, b):
    return lax.dot_general(a, b, (((1,), (0,)), ((), ())), preferred_element_type=F32)


def kernel(
    nd, ntp, blocks, block, rank, held, rows, chunks, ff, feat, tiles,
    g_ref, h_ref, w_ref, a_ref, b_ref, tab, live,
    hg_ref, oa_ref, ob_ref,
    g_all, h_v, w_v, a_all, b_all, a_sel, b_sel, b_in, lo_all, lo_bf, lo_t,
    li_part, li_rs, li_all, li_bf, ga, gb, acc, hg_v, oa_v, ob_v,
    w_sem, own_sem, out_sem,
    nb_s, nb_r, sib_s, sib_r, bdp_s, bdp_r, adp_s, adp_r, bs_s, bs_r,
    lo_s, lo_r, rs_s, rs_r, li_s, li_r, ga_s, ga_r, gb_s, gb_r,
):
    nz = ntp // 2
    dp = lax.axis_index("dp")
    j = lax.axis_index("seqtp")
    z = lax.div(j, 2)
    c = lax.rem(j, 2)
    sib = z * 2 + 1 - c
    crow = rows // chunks
    tile = ff // tiles
    pair = 2 * rows
    piece = blocks * rank // ntp
    fused = pair == block

    def dp_peer(k):
        return lax.rem(dp + k, nd)

    def tp_peer(k):
        return lax.rem(j + k, ntp)

    def dp_from(k):
        return lax.rem(dp + nd - k, nd)

    def tp_from(k):
        return lax.rem(j + ntp - k, ntp)

    def slab(index, size):
        return pl.ds(pl.multiple_of(index * size, size), size)

    w_cp = lambda n: pltpu.make_async_copy(
        w_ref.at[slab(n, tile)], w_v.at[slab(n, tile)], w_sem.at[n]
    )
    own = [
        pltpu.make_async_copy(g_ref, g_all.at[slab(j, rows)], own_sem.at[0]),
        pltpu.make_async_copy(b_ref, b_all.at[pl.ds(dp * held, held)], own_sem.at[1]),
        pltpu.make_async_copy(h_ref, h_v, own_sem.at[2]),
        pltpu.make_async_copy(a_ref, a_all.at[pl.ds(dp * held, held)], own_sem.at[3]),
    ]
    own[0].start()
    own[1].start()
    for n in range(tiles):
        w_cp(n).start()
    own[2].start()
    own[3].start()

    barrier = pltpu.get_barrier_semaphore()
    for k in range(1, nd):
        pl.semaphore_signal(barrier, inc=1, device_id=(dp_peer(k), j), device_id_type=MESH)
    for k in range(1, ntp):
        pl.semaphore_signal(barrier, inc=1, device_id=(dp, tp_peer(k)), device_id_type=MESH)
    pl.semaphore_wait(barrier, nd - 1 + ntp - 1)

    def source(way, d):
        return z - d if way == 0 else z + d

    def has(way, d):
        return z >= d if way == 0 else z + d < nz

    def chunk_at(ref, first, k):
        return ref.at[pl.ds(pl.multiple_of(first + k * crow, crow), crow)]

    def nb_copy(way, d, k):
        first = (source(way, d) * 2 + c) * rows
        src = chunk_at(g_ref, 0, k) if d == 0 else chunk_at(g_all, first, k)
        return pltpu.make_async_remote_copy(
            src_ref=src, dst_ref=chunk_at(g_all, first, k),
            send_sem=nb_s.at[way, d, k], recv_sem=nb_r.at[way, d + 1, k],
            device_id=(dp, j + 2 if way == 0 else j - 2), device_id_type=MESH,
        )

    def nb_arrival(way, d, k):
        first = (source(way, d) * 2 + c) * rows
        here = chunk_at(g_all, first, k)
        return pltpu.make_async_remote_copy(
            src_ref=here, dst_ref=here,
            send_sem=nb_s.at[way, d, k], recv_sem=nb_r.at[way, d, k],
            device_id=(dp, sib), device_id_type=MESH,
        )

    def sib_copy(way, d, k, core):
        first = (source(way, d) * 2 + core) * rows
        src = chunk_at(g_ref, 0, k) if d == 0 else chunk_at(g_all, first, k)
        return pltpu.make_async_remote_copy(
            src_ref=src, dst_ref=chunk_at(g_all, first, k),
            send_sem=sib_s.at[way, d, k], recv_sem=sib_r.at[way, d, k],
            device_id=(dp, sib), device_id_type=MESH,
        )

    def send_on(way, d, k):
        @pl.when(has(way, d) & has(1 - way, 1))
        def _():
            nb_copy(way, d, k).start()

    def receive(d, k):
        for way in (0, 1):
            @pl.when(has(way, d))
            def _():
                nb_arrival(way, d, k).wait_recv()
            if d < nz - 1:
                send_on(way, d, k)

            @pl.when(has(way, d))
            def _():
                sib_copy(way, d, k, c).start()

    half = chunks // 2

    def send_own(lo, hi):
        for k in range(lo, hi):
            send_on(0, 0, k)
            send_on(1, 0, k)
            sib_copy(0, 0, k, c).start()

    send_own(0, half)

    def dp_copy(src, dst, s, r, k):
        return pltpu.make_async_remote_copy(
            src_ref=src, dst_ref=dst, send_sem=s.at[k], recv_sem=r.at[k],
            device_id=(dp_peer(k), j), device_id_type=MESH,
        )

    def tp_copy(src, dst, s, r, k):
        return pltpu.make_async_remote_copy(
            src_ref=src, dst_ref=dst, send_sem=s.at[k], recv_sem=r.at[k],
            device_id=(dp, tp_peer(k)), device_id_type=MESH,
        )

    def b_copy(k, who):
        return dp_copy(b_ref, b_all.at[pl.ds(who * held, held)], bdp_s, bdp_r, k)

    def a_copy(k, who):
        return dp_copy(a_ref, a_all.at[pl.ds(who * held, held)], adp_s, adp_r, k)

    for k in range(1, nd):
        b_copy(k, dp).start()
    for k in range(1, nd):
        a_copy(k, dp).start()

    def block_of(index):
        return lax.div(index * rows, block)

    own[1].wait()
    for k in range(1, nd):
        b_copy(k, dp_from(k)).wait_recv()
    for b in range(blocks):
        b_sel[b] = b_all[tab[dp, b]]
    b_in[j] = b_sel[block_of(j)]

    def bs_copy(k, who, whose):
        return tp_copy(b_sel.at[block_of(whose)], b_in.at[who], bs_s, bs_r, k)

    for k in range(1, ntp):
        bs_copy(k, j, tp_peer(k)).start()
    send_own(half, chunks)

    own[0].wait()
    for k in range(chunks):
        sib_copy(0, 0, k, 1 - c).wait_recv()

    def product(first, size, n):
        return dot_nt(g_all[pl.ds(first, size), :], w_v[slab(n, tile), :])

    def finish(zb, b, n, value):
        cols = slab(n, tile) if tiles > 1 else pl.ds(0, tile)
        filled = live[dp, b]
        keep = (lax.broadcasted_iota(jnp.int32, (block, 1), 0) < filled).astype(F32)
        extra = dot_nn(lo_t[b], a_sel[b, :, cols])
        hg_v[slab(b, block), cols] = (value * keep + adapter_scale * extra).astype(BF16)

    def mm_tiles(zb, lo, hi, final, wait_w):
        def one(n, carry):
            if wait_w:
                w_cp(n).wait()
            first = pl.multiple_of(zb * pair, pair)
            value = product(first, pair, n)
            if final:
                finish(zb, zb, n, value)
            else:
                cols = slab(n, tile) if tiles > 1 else pl.ds(0, tile)
                acc[pl.ds(first, pair), cols] = value
            return carry
        lax.fori_loop(lo, hi, one, 0)

    def fin_tiles(b):
        def one(n, carry):
            cols = slab(n, tile) if tiles > 1 else pl.ds(0, tile)
            finish(b, b, n, acc[slab(b, block), cols])
            return carry
        lax.fori_loop(0, tiles, one, 0)

    def hg_out(zb):
        return pltpu.make_async_copy(
            hg_v.at[slab(zb, block)], hg_ref.at[slab(zb, block)], out_sem.at[2 + zb]
        )

    def step(d, final, start=0, stop=chunks):
        def one(k, carry):
            if d + 1 < nz:
                receive(d + 1, k)
            lo, hi = lax.div(tiles * k, chunks), lax.div(tiles * (k + 1), chunks)
            for way in (0, 1) if d else (0,):
                @pl.when(has(way, d))
                def _():
                    mm_tiles(source(way, d), lo, hi, final, d == 0)
            return carry
        if start < stop:
            lax.fori_loop(start, stop, one, 0)
        if final and stop == chunks:
            for way in (0, 1) if d else (0,):
                @pl.when(has(way, d))
                def _():
                    hg_out(source(way, d)).start()

    def siblings(d):
        for way in (0, 1):
            @pl.when(has(way, d))
            def _():
                for k in range(chunks):
                    sib_copy(way, d, k, 1 - c).wait_recv()

    step(0, False, 0, half)

    for k in range(1, ntp):
        bs_copy(k, tp_from(k), j).wait_recv()
    low = jnp.zeros((rank, rows), F32)
    for s in range(ntp):
        low = low + dot_nt(b_in[s], g_all[slab(j, rows), s * feat : (s + 1) * feat])
    offset = lax.rem(j * rows, block)
    live_here = lax.broadcasted_iota(jnp.int32, (rank, rows), 1) + offset < live[dp, block_of(j)]
    low = (low * live_here.astype(F32)).astype(BF16)
    place = (
        lax.broadcasted_iota(jnp.int32, (rows, block), 1)
        == lax.broadcasted_iota(jnp.int32, (rows, block), 0) + offset
    ).astype(F32).astype(BF16)
    lo_all[j] = dot_nn(low, place).astype(BF16)

    def lo_copy(k, who):
        return tp_copy(lo_all.at[who], lo_all.at[who], lo_s, lo_r, k)

    for k in range(1, ntp):
        lo_copy(k, j).start()

    step(0, False, half)

    own[2].wait()
    for k in range(1, ntp):
        lo_copy(k, tp_from(k)).wait_recv()
    per_block = block // rows
    for b in range(blocks):
        value = lo_all[b * per_block].astype(F32)
        for s in range(1, per_block):
            value = value + lo_all[b * per_block + s].astype(F32)
        lo_bf[b] = value.astype(BF16)
        lo_t[b] = value.T.astype(BF16)
        ga[dp, b * rank : (b + 1) * rank, :] = (
            adapter_scale * dot_nn(lo_bf[b], h_v[b * block : (b + 1) * block, :])
        ).astype(BF16)

    def ga_copy(k, who):
        return dp_copy(ga.at[who], ga.at[who], ga_s, ga_r, k)

    def gb_copy(k, who):
        return dp_copy(gb.at[who], gb.at[who], gb_s, gb_r, k)

    for k in range(1, nd):
        ga_copy(k, dp).start()

    siblings(1)
    step(1, False, 0, half)

    own[3].wait()
    for k in range(1, nd):
        a_copy(k, dp_from(k)).wait_recv()
    for b in range(blocks):
        a_sel[b] = a_all[tab[dp, b]]
        value = dot_nt(a_sel[b], h_v[b * block : (b + 1) * block, :])
        for i in range(rank // piece):
            li_part[b * (rank // piece) + i] = value[i * piece : (i + 1) * piece, :]
    li_rs[j] = li_part[j]

    def rs_copy(k, who, whose):
        return tp_copy(li_part.at[whose], li_rs.at[who], rs_s, rs_r, k)

    for k in range(1, ntp):
        rs_copy(k, j, tp_peer(k)).start()

    step(1, False, half)

    for k in range(1, ntp):
        rs_copy(k, tp_from(k), j).wait_recv()
    total = li_rs[0]
    for s in range(1, ntp):
        total = total + li_rs[s]
    li_all[j] = total

    def li_copy(k, who):
        return tp_copy(li_all.at[who], li_all.at[who], li_s, li_r, k)

    for k in range(1, ntp):
        li_copy(k, j).start()

    if fused:
        for d in (0, 1):
            for way in (0, 1) if d else (0,):
                @pl.when(has(way, d))
                def _():
                    fin_tiles(source(way, d))
                    hg_out(source(way, d)).start()

    siblings(2)
    step(2, fused, 0, half)

    for k in range(1, ntp):
        li_copy(k, tp_from(k)).wait_recv()
    group = rank // piece
    for b in range(blocks):
        value = jnp.concatenate([li_all[b * group + i] for i in range(group)], axis=0)
        keep = lax.broadcasted_iota(jnp.int32, (rank, block), 1) < live[dp, b]
        li_bf[b] = (value * keep.astype(F32)).astype(BF16)

    def gb_block(b):
        gb[dp, slab(b, rank), :] = (
            adapter_scale * dot_nn(li_bf[b], g_all[slab(b, block), slab(j, feat)])
        ).astype(BF16)

    def gb_blocks(d):
        for way in (0, 1) if d else (0,):
            @pl.when(has(way, d))
            def _():
                gb_block(source(way, d))

    if fused:
        for d in range(nz - 1):
            gb_blocks(d)

    def chooser(g):
        r = lax.broadcasted_iota(jnp.int32, (held * rank, blocks * rank), 0)
        q = lax.broadcasted_iota(jnp.int32, (held * rank, blocks * rank), 1)
        same = (r & (rank - 1)) == (q & (rank - 1))
        which = jnp.zeros_like(q)
        for b in range(blocks):
            lane = (q >= b * rank) & (q < (b + 1) * rank)
            which = jnp.where(lane, tab[g, b] - dp * held, which)
        hit = (r >= which * rank) & (r < (which + 1) * rank) & same
        return hit.astype(F32).astype(BF16)

    picks = [chooser(g) for g in range(nd)]
    for k in range(1, nd):
        ga_copy(k, dp_from(k)).wait_recv()
    total = dot_nn(picks[0], ga[0])
    for g in range(1, nd):
        total = total + dot_nn(picks[g], ga[g])
    oa_v[...] = total.reshape(held, rank, ff)
    oa_cp = pltpu.make_async_copy(oa_v, oa_ref, out_sem.at[0])
    oa_cp.start()
    step(2, fused, half)
    for d in range(3, nz - 1):
        siblings(d)
        step(d, fused)

    siblings(nz - 1)
    if fused:
        gb_blocks(nz - 1)
    else:
        for b in range(blocks):
            gb_block(b)
    for k in range(1, nd):
        gb_copy(k, dp).start()

    step(nz - 1, fused)
    if not fused:
        for b in range(blocks):
            fin_tiles(b)
            hg_out(b).start()

    for k in range(1, nd):
        gb_copy(k, dp_from(k)).wait_recv()
    total = dot_nn(picks[0], gb[0])
    for g in range(1, nd):
        total = total + dot_nn(picks[g], gb[g])
    ob_v[...] = total.reshape(held, rank, feat)
    ob_cp = pltpu.make_async_copy(ob_v, ob_ref, out_sem.at[1])
    ob_cp.start()

    for d in range(nz):
        for way in (0, 1):
            if d < nz - 1:
                @pl.when(has(way, d) & has(1 - way, 1))
                def _():
                    for k in range(chunks):
                        nb_copy(way, d, k).wait_send()
            if d or way == 0:
                @pl.when(has(way, d))
                def _():
                    for k in range(chunks):
                        sib_copy(way, d, k, c).wait_send()
    for k in range(1, nd):
        for copy in (b_copy, a_copy, ga_copy, gb_copy):
            copy(k, dp).wait_send()
    for k in range(1, ntp):
        bs_copy(k, j, tp_peer(k)).wait_send()
        rs_copy(k, j, tp_peer(k)).wait_send()
        lo_copy(k, j).wait_send()
        li_copy(k, j).wait_send()
    for b in range(blocks):
        hg_out(b).wait()
    oa_cp.wait()
    ob_cp.wait()


def copy_kernel(blocks, hg, oa, ob, hg_out, oa_out, ob_out, hg_v, oa_v, ob_v, in_sem, out_sem):
    size = hg.shape[0] // blocks
    stages = [
        tuple(ref.at[pl.ds(b * size, size)] for ref in (hg, hg_v, hg_out)) for b in range(blocks)
    ] + [(oa, oa_v, oa_out), (ob, ob_v, ob_out)]
    loads = [pltpu.make_async_copy(s, v, in_sem.at[i]) for i, (s, v, _) in enumerate(stages)]
    stores = [pltpu.make_async_copy(v, o, out_sem.at[i]) for i, (_, v, o) in enumerate(stages)]
    for load in loads:
        load.start()
    for load, store in zip(loads, stores):
        load.wait()
        store.start()
    for store in stores:
        store.wait()


def shards(nd, ntp, g, h, w, a, bm, tab, live):
    blocks = tab.shape[1]
    group_rows, ff = h.shape
    block = group_rows // blocks
    held, rank, _ = a.shape
    feat = bm.shape[2]
    rows, width = g.shape
    nz = ntp // 2
    chunks = max(1, min(2, rows // 16))
    tiles = ff // 256 if ff % 256 == 0 else 1
    piece = blocks * rank // ntp
    V = pltpu.VMEM
    dma = lambda *s: pltpu.SemaphoreType.DMA(s)
    scratch = [
        V((group_rows, width), BF16), V((group_rows, ff), BF16), V((ff, width), BF16),
        V((nd * held, rank, ff), BF16), V((nd * held, rank, feat), BF16),
        V((blocks, rank, ff), BF16), V((blocks, rank, feat), BF16),
        V((ntp, rank, feat), BF16), V((ntp, rank, block), BF16),
        V((blocks, rank, block), BF16), V((blocks, block, rank), BF16),
        V((ntp, piece, block), F32), V((ntp, piece, block), F32), V((ntp, piece, block), F32),
        V((blocks, rank, block), BF16),
        V((nd, blocks * rank, ff), BF16), V((nd, blocks * rank, feat), BF16),
        V((group_rows, ff), F32), V((group_rows, ff), BF16),
        V((held, rank, ff), F32), V((held, rank, feat), F32),
        dma(tiles), dma(4), dma(2 + blocks),
        dma(2, nz, chunks), dma(2, nz + 1, chunks), dma(2, nz, chunks), dma(2, nz, chunks),
        dma(nd), dma(nd), dma(nd), dma(nd), dma(ntp), dma(ntp),
        dma(ntp), dma(ntp), dma(ntp), dma(ntp), dma(ntp), dma(ntp),
        dma(nd), dma(nd), dma(nd), dma(nd),
    ]
    any_spec = pl.BlockSpec(memory_space=pl.ANY)
    smem = pl.BlockSpec(memory_space=pltpu.SMEM)
    hg, oa, ob = pl.pallas_call(
        functools.partial(
            kernel, nd, ntp, blocks, block, rank, held, rows, chunks, ff, feat, tiles
        ),
        out_shape=(
            jax.ShapeDtypeStruct((group_rows, ff), BF16),
            jax.ShapeDtypeStruct((held, rank, ff), F32),
            jax.ShapeDtypeStruct((held, rank, feat), F32),
        ),
        in_specs=[any_spec] * 5 + [smem] * 2,
        out_specs=(any_spec,) * 3,
        scratch_shapes=scratch,
        compiler_params=pltpu.CompilerParams(
            collective_id=0, has_side_effects=True, vmem_limit_bytes=62 * 1024 * 1024
        ),
    )(g, h, w, a, bm, tab, live)
    results = (hg, oa, ob)
    return pl.pallas_call(
        functools.partial(copy_kernel, blocks),
        out_shape=tuple(jax.ShapeDtypeStruct(x.shape, x.dtype) for x in results),
        in_specs=[any_spec] * 3,
        out_specs=(any_spec,) * 3,
        scratch_shapes=[V(x.shape, x.dtype) for x in results] + [dma(blocks + 2), dma(blocks + 2)],
        compiler_params=pltpu.CompilerParams(vmem_limit_bytes=62 * 1024 * 1024),
    )(*results)


def line_kernel(
    nd, nz, blocks, block, rank, held, rows, sizes, ff, feat, width,
    g_ref, h_ref, w_ref, a_ref, b_ref, tab, live,
    hg_v, oa_v, ob_v,
    g_all, h_v, w_v, a_own, b_own, a_out, b_out, a_in, b_from, a_sel, b_sel, b_in,
    lo_part, lo_all, lo_t, li_part, li_sib, li_sum, li_rs, li_all, ga, gb, acc,
    w_sem, own_sem, relay,
    nb_s, nb_r, sib_s, sib_r, row_s, row_r, bdp_s, bdp_r, adp_s, adp_r,
    bs_s, bs_r, lo_s, lo_r, rs_s, rs_r, ag_s, ag_r, pair_s, pair_r,
    ga_s, ga_r, gb_s, gb_r,
):
    dp = lax.axis_index("dp")
    j = lax.axis_index("seqtp")
    z = lax.div(j, 2)
    c = lax.rem(j, 2)
    sib = z * 2 + 1 - c
    chunks = len(sizes)
    tile = 256
    tiles = ff // tile
    piece = blocks * rank // (2 * nz)
    pair_rows = 2 * block
    near = lax.div(z, 2)
    far = 1 - near
    starts = [sum(sizes[:i]) for i in range(chunks)]

    def slab(index, size):
        return pl.ds(pl.multiple_of(index * size, size), size)

    def has(way, d):
        return z >= d if way == 0 else z + d < nz

    def source(way, d):
        return z - d if way == 0 else z + d

    def dp_peer(k):
        return lax.rem(dp + k, nd)

    def dp_from(k):
        return lax.rem(dp + nd - k, nd)

    def z_peer(k):
        return lax.rem(z + k, nz)

    def z_from(k):
        return lax.rem(z + nz - k, nz)

    def toward(way):
        return (dp, j + 2 if way == 0 else j - 2)

    barrier = pltpu.get_barrier_semaphore()
    for way in (0, 1):
        @pl.when(has(1 - way, 1))
        def _():
            pl.semaphore_signal(barrier, inc=1, device_id=toward(way), device_id_type=MESH)
    pl.semaphore_signal(barrier, inc=1, device_id=(dp, sib), device_id_type=MESH)
    for k in range(1, nd):
        pl.semaphore_signal(barrier, inc=1, device_id=(dp_peer(k), j), device_id_type=MESH)

    own = [
        pltpu.make_async_copy(b_ref, b_own, own_sem.at[0]),
        pltpu.make_async_copy(g_ref, g_all.at[slab(j, rows)], own_sem.at[1]),
        pltpu.make_async_copy(h_ref, h_v, own_sem.at[2]),
        pltpu.make_async_copy(a_ref, a_own, own_sem.at[3]),
    ]
    w_cp = [
        pltpu.make_async_copy(w_ref.at[pl.ds(n * tile, tile)], w_v.at[pl.ds(n * tile, tile)], w_sem.at[n])
        for n in range(tiles)
    ]
    own[0].start()
    own[3].start()
    own[1].start()

    @pl.when(has(0, 1) & has(1, 1))
    def _():
        pl.semaphore_wait(barrier, nd + 2)

    @pl.when(jnp.logical_not(has(0, 1) & has(1, 1)))
    def _():
        pl.semaphore_wait(barrier, nd + 1)

    def part(ref, first, way, i):
        start = starts[i] if way == 1 else width - starts[i] - sizes[i]
        return ref.at[slab(first, rows), pl.ds(start, sizes[i])]

    def nb_copy(way, d, i):
        first = source(way, d) * 2 + c
        src = part(g_ref, 0, way, i) if d == 0 else part(g_all, first, way, i)
        return pltpu.make_async_remote_copy(
            src_ref=src, dst_ref=part(g_all, first, way, i),
            send_sem=nb_s.at[way, d, i], recv_sem=nb_r.at[way, d + 1, i],
            device_id=toward(way), device_id_type=MESH,
        )

    def nb_arrival(way, d, i):
        here = part(g_all, source(way, d) * 2 + c, way, i)
        return pltpu.make_async_remote_copy(
            src_ref=here, dst_ref=here,
            send_sem=nb_s.at[way, d - 1, i], recv_sem=nb_r.at[way, d, i],
            device_id=(dp, sib), device_id_type=MESH,
        )

    def sib_copy(way, d, i, core):
        here = part(g_all, source(way, d) * 2 + core, way, i)
        return pltpu.make_async_remote_copy(
            src_ref=here, dst_ref=here,
            send_sem=sib_s.at[way, d, i], recv_sem=sib_r.at[way, d, i],
            device_id=(dp, sib), device_id_type=MESH,
        )

    def row_copy(index):
        return pltpu.make_async_remote_copy(
            src_ref=g_ref, dst_ref=g_all.at[slab(index, rows)],
            send_sem=row_s, recv_sem=row_r, device_id=(dp, sib), device_id_type=MESH,
        )

    def onward(way, d):
        return has(way, d) & has(1 - way, 1)

    def advance(n):
        d, i = n // chunks, n % chunks
        if d < nz - 1:
            for way in (0, 1):
                @pl.when(onward(way, d))
                def _():
                    nb_copy(way, d, i).start()

    def event(n):
        d, i = n // chunks, n % chunks
        for way in (0, 1):
            @pl.when(has(way, d + 1))
            def _():
                nb_arrival(way, d + 1, i).wait_recv()
                sib_copy(way, d + 1, i, c).start()
        for way in (0, 1):
            @pl.when(onward(way, d))
            def _():
                nb_copy(way, d, i).wait_send()

    def landed(n):
        d, i = n // chunks + 1, n % chunks
        for way in (0, 1):
            @pl.when(has(way, d))
            def _():
                sib_copy(way, d, i, 1 - c).wait_recv()

    def dp_copy(src, dst, s, r, k):
        return pltpu.make_async_remote_copy(
            src_ref=src, dst_ref=dst, send_sem=s.at[k], recv_sem=r.at[k],
            device_id=(dp_peer(k), j), device_id_type=MESH,
        )

    def z_copy(src, dst, s, r, k):
        return pltpu.make_async_remote_copy(
            src_ref=src, dst_ref=dst, send_sem=s.at[k], recv_sem=r.at[k],
            device_id=(dp, z_peer(k) * 2 + c), device_id_type=MESH,
        )

    def core_copy(src, dst, k):
        return pltpu.make_async_remote_copy(
            src_ref=src, dst_ref=dst, send_sem=pair_s.at[k], recv_sem=pair_r.at[k],
            device_id=(dp, sib), device_id_type=MESH,
        )

    def b_copy(k, who):
        return dp_copy(b_out.at[k], b_from.at[who], bdp_s, bdp_r, k)

    def a_copy(k, who):
        return dp_copy(a_out.at[k], a_in.at[who], adp_s, adp_r, k)

    def at_owner(group, b):
        return jnp.clip(tab[group, b] - dp * held, 0, held - 1)

    def bs_copy(k, who, whose):
        return z_copy(b_sel.at[whose], b_in.at[who], bs_s, bs_r, k)

    def lo_copy(k, who):
        return z_copy(lo_all.at[who], lo_all.at[who], lo_s, lo_r, k)

    def rs_copy(k, who, whose):
        return z_copy(li_sum.at[whose], li_rs.at[who], rs_s, rs_r, k)

    def ag_copy(k, who):
        return z_copy(li_all.at[c * nz + who], li_all.at[c * nz + who], ag_s, ag_r, k)

    def ga_copy(k, who):
        return dp_copy(ga.at[who], ga.at[who], ga_s, ga_r, k)

    def gb_copy(k, who):
        return dp_copy(gb.at[who], gb.at[who], gb_s, gb_r, k)

    def lo_pair(core):
        return core_copy(lo_part.at[core], lo_part.at[core], 0)

    def li_pair(core):
        return core_copy(li_part.at[1 - core], li_sib, 1)

    def ag_pair(core):
        here = li_all.at[pl.ds(core * nz, nz)]
        return core_copy(here, here, 2)

    advance(0)
    advance(1)
    advance(2)
    row_copy(j).start()
    own[0].wait()
    for k in range(1, nd):
        for b in range(blocks):
            b_out[k, b] = b_own[at_owner(dp_peer(k), b)]
        b_copy(k, dp).start()
    for b in range(blocks):
        b_from[dp, b] = b_own[at_owner(dp, b)]
    for way in (0, 1):
        @pl.when(has(way, 1) & has(1 - way, 1))
        def _():
            pl.semaphore_signal(relay.at[way, 2], inc=1, device_id=toward(way), device_id_type=MESH)
    own[2].start()
    for n in range(tiles):
        w_cp[n].start()
    own[3].wait()
    for k in range(1, nd):
        for b in range(blocks):
            a_out[k, b] = a_own[at_owner(dp_peer(k), b)]
        a_copy(k, dp).start()
    for b in range(blocks):
        a_in[dp, b] = a_own[at_owner(dp, b)]

    for d in range(2, nz):
        for way in (0, 1):
            @pl.when(has(way, d))
            def _():
                pl.semaphore_wait(relay.at[way, d], 1)
                if d + 1 < nz:
                    @pl.when(has(1 - way, 1))
                    def _():
                        pl.semaphore_signal(
                            relay.at[way, d + 1], inc=1, device_id=toward(way), device_id_type=MESH
                        )

    for k in range(1, nd):
        b_copy(k, dp_from(k)).wait_recv()
    for b in range(blocks):
        b_sel[b] = b_from[lax.div(tab[dp, b], held), b]
    b_in[z] = b_sel[z]
    for k in range(1, nz):
        bs_copy(k, z, z_peer(k)).start()

    event(0)
    advance(3)
    event(1)
    advance(4)

    own[1].wait()
    row_copy(sib).wait_recv()
    for k in range(1, nz):
        bs_copy(k, z_from(k), z).wait_recv()
    low = jnp.zeros((rank, block), F32)
    for s in range(nz):
        low = low + dot_nt(b_in[s], g_all[slab(z, block), slab(2 * s + c, feat)])
    lo_part[c] = low
    lo_pair(c).start()

    event(2)

    lo_pair(1 - c).wait_recv()
    lanes = lax.broadcasted_iota(jnp.int32, (rank, block), 1)
    low = lo_part[0] + lo_part[1]
    lo_all[z] = (low * (lanes < live[dp, z]).astype(F32)).astype(BF16)
    for k in range(1, nz):
        lo_copy(k, z).start()
    advance(5)

    event(3)
    advance(6)
    event(4)
    advance(7)

    own[2].wait()
    for k in range(1, nz):
        lo_copy(k, z_from(k)).wait_recv()
    for b in range(blocks):
        lo_t[b] = lo_all[b].astype(F32).T.astype(BF16)
        ga[dp, b * rank : (b + 1) * rank, :] = (
            adapter_scale * dot_nn(lo_all[b], h_v[b * block : (b + 1) * block, :])
        ).astype(BF16)
    for k in range(1, nd):
        ga_copy(k, dp).start()

    for k in range(1, nd):
        a_copy(k, dp_from(k)).wait_recv()
    for b in range(blocks):
        a_sel[b] = a_in[lax.div(tab[dp, b], held), b]
        value = dot_nt(a_sel[b], h_v[b * block : (b + 1) * block, :])
        for i in range(rank // piece):
            at = b * (rank // piece) + i
            li_part[at // nz, at % nz] = value[i * piece : (i + 1) * piece, :]
    li_pair(c).start()

    def keep_of(b):
        return (lax.broadcasted_iota(jnp.int32, (block, 1), 0) < live[dp, b]).astype(F32)

    for n in range(chunks):
        landed(n)
    for n in range(tiles):
        w_cp[n].wait()

    def near_tiles(lo, hi):
        def one(n, carry):
            cols = slab(n, tile)
            value = dot_nt(g_all[slab(near, pair_rows), :], w_v[slab(n, tile), :])
            for s in range(2):
                b = near * 2 + s
                extra = dot_nn(lo_t[b], a_sel[b, :, cols])
                total = value[s * block : (s + 1) * block] + adapter_scale * extra
                hg_v[slab(b, block), cols] = (total * keep_of(b)).astype(BF16)
            return carry
        lax.fori_loop(lo, hi, one, 0)

    near_tiles(0, 1)
    event(5)

    li_pair(1 - c).wait_recv()
    li_sum[...] = li_part[c] + li_sib[...]
    li_rs[z] = li_sum[z]
    for k in range(1, nz):
        rs_copy(k, z, z_peer(k)).start()
    advance(8)

    near_tiles(1, 3)
    event(6)
    advance(9)
    near_tiles(3, 5)
    event(7)

    for k in range(1, nz):
        rs_copy(k, z_from(k), z).wait_recv()
    total = li_rs[0]
    for s in range(1, nz):
        total = total + li_rs[s]
    whole = c * nz + z
    lanes = lax.broadcasted_iota(jnp.int32, (piece, block), 1)
    filled = live[dp, lax.div(whole * piece, rank)]
    li_all[whole] = (total * (lanes < filled).astype(F32)).astype(BF16)
    for k in range(1, nz):
        ag_copy(k, z).start()
    advance(10)
    near_tiles(5, tiles)

    def gb_block(b):
        group = rank // piece
        rows_of = jnp.concatenate(
            [li_all[b * group + i].astype(F32) for i in range(group)], axis=0
        ).astype(BF16)
        gb[dp, slab(b, rank), :] = (
            adapter_scale * dot_nn(rows_of, g_all[slab(b, block), slab(j, feat)])
        ).astype(BF16)

    def chooser(g):
        r = lax.broadcasted_iota(jnp.int32, (held * rank, blocks * rank), 0)
        q = lax.broadcasted_iota(jnp.int32, (held * rank, blocks * rank), 1)
        same = (r & (rank - 1)) == (q & (rank - 1))
        which = jnp.zeros_like(q)
        for b in range(blocks):
            lane = (q >= b * rank) & (q < (b + 1) * rank)
            which = jnp.where(lane, tab[g, b] - dp * held, which)
        hit = (r >= which * rank) & (r < (which + 1) * rank) & same
        return hit.astype(F32).astype(BF16)

    def owned(ref):
        total = dot_nn(chooser(0), ref[0])
        for g in range(1, nd):
            total = total + dot_nn(chooser(g), ref[g])
        return total


    for s in range(2):
        b = far * 2 + s
        acc[s * block : (s + 1) * block, :] = adapter_scale * dot_nn(lo_t[b], a_sel[b])

    def drain(d):
        for way in (0, 1):
            for i in range(chunks):
                if d:
                    @pl.when(has(way, d))
                    def _():
                        sib_copy(way, d, i, c).wait_send()

    row_copy(j).wait_send()
    drain(1)
    for k in range(1, nd):
        for copy in (b_copy, a_copy):
            copy(k, dp).wait_send()
    for k in range(1, nz):
        bs_copy(k, z, z_peer(k)).wait_send()
        lo_copy(k, z).wait_send()
        rs_copy(k, z, z_peer(k)).wait_send()
    for copy in (lo_pair, li_pair):
        copy(c).wait_send()
    for n in range(chunks, 2 * chunks):
        landed(n)

    def far_chunk(i, last):
        start = jnp.where(z < nz // 2, starts[i], width - starts[i] - sizes[i])
        deep = pl.ds(pl.multiple_of(start, 128), sizes[i])
        keep = jnp.concatenate([keep_of(far * 2 + s) for s in range(2)], axis=0) if last else None
        rows_at = slab(far, pair_rows)
        for n in range(tiles):
            cols = pl.ds(n * tile, tile)
            value = acc[:, cols] + dot_nt(g_all[rows_at, deep], w_v[cols, deep])
            if last:
                hg_v[rows_at, cols] = (value * keep).astype(BF16)
            else:
                acc[:, cols] = value

    for i in range(chunks):
        event(2 * chunks + i)
        advance(2 * chunks + i + 3)
        landed(2 * chunks + i)
        far_chunk(i, i == chunks - 1)
        if i == 0:
            for k in range(1, nz):
                ag_copy(k, z_from(k)).wait_recv()
            ag_pair(c).start()
            for k in range(1, nd):
                ga_copy(k, dp_from(k)).wait_recv()
            oa_v[...] = owned(ga).reshape(held, rank, ff)
            ag_pair(1 - c).wait_recv()
            for b in range(blocks):
                gb_block(b)
            for k in range(1, nd):
                gb_copy(k, dp).start()
        if i == chunks - 2:
            for k in range(1, nd):
                gb_copy(k, dp_from(k)).wait_recv()
            ob_v[...] = owned(gb).reshape(held, rank, feat)
            for k in range(1, nd):
                gb_copy(k, dp).wait_send()
                ga_copy(k, dp).wait_send()
            for k in range(1, nz):
                ag_copy(k, z).wait_send()
            ag_pair(c).wait_send()
            drain(2)
    for d in range(3, nz):
        drain(d)


def store_kernel(blocks, hg, oa, ob, hg_out, oa_out, ob_out, sem):
    size = hg.shape[0] // blocks
    copies = [
        (hg.at[pl.ds(b * size, size)], hg_out.at[pl.ds(b * size, size)]) for b in range(blocks)
    ] + [(oa, oa_out), (ob, ob_out)]
    copies = [pltpu.make_async_copy(s, o, sem.at[i]) for i, (s, o) in enumerate(copies)]
    for copy in copies:
        copy.start()
    for copy in copies:
        copy.wait()


def line_shards(nd, ntp, g, h, w, a, bm, tab, live):
    blocks = tab.shape[1]
    group_rows, ff = h.shape
    block = group_rows // blocks
    held, rank, _ = a.shape
    feat = bm.shape[2]
    rows, width = g.shape
    nz = ntp // 2
    sizes = (width // 4,) * 4
    tiles = ff // 256
    chunks = len(sizes)
    piece = blocks * rank // ntp
    V = pltpu.VMEM
    dma = lambda *s: pltpu.SemaphoreType.DMA(s)
    scratch = [
        V((group_rows, width), BF16), V((group_rows, ff), BF16), V((ff, width), BF16),
        V((held, rank, ff), BF16), V((held, rank, feat), BF16),
        V((nd, blocks, rank, ff), BF16), V((nd, blocks, rank, feat), BF16),
        V((nd, blocks, rank, ff), BF16), V((nd, blocks, rank, feat), BF16),
        V((blocks, rank, ff), BF16), V((blocks, rank, feat), BF16), V((nz, rank, feat), BF16),
        V((2, rank, block), F32), V((blocks, rank, block), BF16), V((blocks, block, rank), BF16),
        V((2, nz, piece, block), F32), V((nz, piece, block), F32), V((nz, piece, block), F32),
        V((nz, piece, block), F32), V((ntp, piece, block), BF16),
        V((nd, blocks * rank, ff), BF16), V((nd, blocks * rank, feat), BF16),
        V((2 * block, ff), F32),
        dma(tiles), dma(4), pltpu.SemaphoreType.REGULAR((2, nz)),
        dma(2, nz, chunks), dma(2, nz + 1, chunks), dma(2, nz, chunks), dma(2, nz, chunks),
        pltpu.SemaphoreType.DMA, pltpu.SemaphoreType.DMA,
        dma(nd), dma(nd), dma(nd), dma(nd),
        dma(nz), dma(nz), dma(nz), dma(nz), dma(nz), dma(nz), dma(nz), dma(nz), dma(3), dma(3),
        dma(nd), dma(nd), dma(nd), dma(nd),
    ]
    hbm = pl.BlockSpec(memory_space=pltpu.HBM)
    smem = pl.BlockSpec(memory_space=pltpu.SMEM)
    vmem = pl.BlockSpec(memory_space=pltpu.VMEM)
    results = pl.pallas_call(
        functools.partial(
            line_kernel, nd, nz, blocks, block, rank, held, rows, sizes, ff, feat, width
        ),
        out_shape=(
            V((group_rows, ff), BF16), V((held, rank, ff), F32), V((held, rank, feat), F32),
        ),
        in_specs=[hbm] * 5 + [smem] * 2,
        out_specs=(vmem,) * 3,
        scratch_shapes=scratch,
        compiler_params=pltpu.CompilerParams(
            collective_id=1, has_side_effects=True, vmem_limit_bytes=61 * 1024 * 1024
        ),
    )(g, h, w, a, bm, tab, live)
    return pl.pallas_call(
        functools.partial(store_kernel, blocks),
        out_shape=tuple(jax.ShapeDtypeStruct(x.shape, x.dtype) for x in results),
        in_specs=[vmem] * 3,
        out_specs=(hbm,) * 3,
        scratch_shapes=[dma(blocks + 2)],
        compiler_params=pltpu.CompilerParams(vmem_limit_bytes=8 * 1024 * 1024),
    )(*results)


def body(nd, ntp, g, h, w, a, bm, tab, live):
    blocks = tab.shape[1]
    group_rows, ff = h.shape
    rows, width = g.shape
    line = (
        ntp == 8 and blocks == 4 and 8 * rows == group_rows and ff % 256 == 0
        and width == ntp * bm.shape[2] and bm.shape[2] % 128 == 0
        and blocks * a.shape[1] == 8 * ntp
    )
    return (line_shards if line else shards)(nd, ntp, g, h, w, a, bm, tab, live)


def solution(mesh):
    in_specs = (
        P(("dp", "seqtp"), None),
        P("dp", "seqtp"),
        P("seqtp", None),
        P("dp", None, "seqtp"),
        P("dp", None, "seqtp"),
        P(),
        P(),
    )
    out_specs = (P("dp", "seqtp"), P("dp", None, "seqtp"), P("dp", None, "seqtp"))
    step = functools.partial(body, mesh.shape["dp"], mesh.shape["seqtp"])
    return jax.shard_map(step, mesh=mesh, in_specs=in_specs, out_specs=out_specs, check_vma=False)
```

```python
import functools

import jax
import jax.numpy as jnp
from jax import lax
from jax.experimental import pallas as pl
from jax.experimental.pallas import tpu as pltpu
from jax.sharding import PartitionSpec as P

adapter_scale = 0.5
MESH = pl.DeviceIdType.MESH
F32 = jnp.float32
BF16 = jnp.bfloat16


def dot_nt(a, b):
    return lax.dot_general(a, b, (((1,), (1,)), ((), ())), preferred_element_type=F32)


def dot_nn(a, b):
    return lax.dot_general(a, b, (((1,), (0,)), ((), ())), preferred_element_type=F32)


def kernel(
    nd, ntp, blocks, block, rank, held, rows, chunks, ff, feat, tiles,
    g_ref, h_ref, w_ref, a_ref, b_ref, tab, live,
    hg_ref, oa_ref, ob_ref,
    g_all, h_v, w_v, a_all, b_all, a_sel, b_sel, b_in, lo_all, lo_bf, lo_t,
    li_part, li_rs, li_all, li_bf, ga, gb, acc, hg_v, oa_v, ob_v,
    w_sem, own_sem, out_sem,
    nb_s, nb_r, sib_s, sib_r, bdp_s, bdp_r, adp_s, adp_r, bs_s, bs_r,
    lo_s, lo_r, rs_s, rs_r, li_s, li_r, ga_s, ga_r, gb_s, gb_r,
):
    nz = ntp // 2
    dp = lax.axis_index("dp")
    j = lax.axis_index("seqtp")
    z = lax.div(j, 2)
    c = lax.rem(j, 2)
    sib = z * 2 + 1 - c
    crow = rows // chunks
    tile = ff // tiles
    pair = 2 * rows
    piece = blocks * rank // ntp
    fused = pair == block

    def dp_peer(k):
        return lax.rem(dp + k, nd)

    def tp_peer(k):
        return lax.rem(j + k, ntp)

    def dp_from(k):
        return lax.rem(dp + nd - k, nd)

    def tp_from(k):
        return lax.rem(j + ntp - k, ntp)

    def slab(index, size):
        return pl.ds(pl.multiple_of(index * size, size), size)

    w_cp = lambda n: pltpu.make_async_copy(
        w_ref.at[slab(n, tile)], w_v.at[slab(n, tile)], w_sem.at[n]
    )
    own = [
        pltpu.make_async_copy(g_ref, g_all.at[slab(j, rows)], own_sem.at[0]),
        pltpu.make_async_copy(b_ref, b_all.at[pl.ds(dp * held, held)], own_sem.at[1]),
        pltpu.make_async_copy(h_ref, h_v, own_sem.at[2]),
        pltpu.make_async_copy(a_ref, a_all.at[pl.ds(dp * held, held)], own_sem.at[3]),
    ]
    own[0].start()
    own[1].start()
    for n in range(tiles):
        w_cp(n).start()
    own[2].start()
    own[3].start()

    barrier = pltpu.get_barrier_semaphore()
    for k in range(1, nd):
        pl.semaphore_signal(barrier, inc=1, device_id=(dp_peer(k), j), device_id_type=MESH)
    for k in range(1, ntp):
        pl.semaphore_signal(barrier, inc=1, device_id=(dp, tp_peer(k)), device_id_type=MESH)
    pl.semaphore_wait(barrier, nd - 1 + ntp - 1)

    def source(way, d):
        return z - d if way == 0 else z + d

    def has(way, d):
        return z >= d if way == 0 else z + d < nz

    def chunk_at(ref, first, k):
        return ref.at[pl.ds(pl.multiple_of(first + k * crow, crow), crow)]

    def nb_copy(way, d, k):
        first = (source(way, d) * 2 + c) * rows
        src = chunk_at(g_ref, 0, k) if d == 0 else chunk_at(g_all, first, k)
        return pltpu.make_async_remote_copy(
            src_ref=src, dst_ref=chunk_at(g_all, first, k),
            send_sem=nb_s.at[way, d, k], recv_sem=nb_r.at[way, d + 1, k],
            device_id=(dp, j + 2 if way == 0 else j - 2), device_id_type=MESH,
        )

    def nb_arrival(way, d, k):
        first = (source(way, d) * 2 + c) * rows
        here = chunk_at(g_all, first, k)
        return pltpu.make_async_remote_copy(
            src_ref=here, dst_ref=here,
            send_sem=nb_s.at[way, d, k], recv_sem=nb_r.at[way, d, k],
            device_id=(dp, sib), device_id_type=MESH,
        )

    def sib_copy(way, d, k, core):
        first = (source(way, d) * 2 + core) * rows
        src = chunk_at(g_ref, 0, k) if d == 0 else chunk_at(g_all, first, k)
        return pltpu.make_async_remote_copy(
            src_ref=src, dst_ref=chunk_at(g_all, first, k),
            send_sem=sib_s.at[way, d, k], recv_sem=sib_r.at[way, d, k],
            device_id=(dp, sib), device_id_type=MESH,
        )

    def send_on(way, d, k):
        @pl.when(has(way, d) & has(1 - way, 1))
        def _():
            nb_copy(way, d, k).start()

    def receive(d, k):
        for way in (0, 1):
            @pl.when(has(way, d))
            def _():
                nb_arrival(way, d, k).wait_recv()
            if d < nz - 1:
                send_on(way, d, k)

            @pl.when(has(way, d))
            def _():
                sib_copy(way, d, k, c).start()

    half = chunks // 2

    def send_own(lo, hi):
        for k in range(lo, hi):
            send_on(0, 0, k)
            send_on(1, 0, k)
            sib_copy(0, 0, k, c).start()

    send_own(0, half)

    def dp_copy(src, dst, s, r, k):
        return pltpu.make_async_remote_copy(
            src_ref=src, dst_ref=dst, send_sem=s.at[k], recv_sem=r.at[k],
            device_id=(dp_peer(k), j), device_id_type=MESH,
        )

    def tp_copy(src, dst, s, r, k):
        return pltpu.make_async_remote_copy(
            src_ref=src, dst_ref=dst, send_sem=s.at[k], recv_sem=r.at[k],
            device_id=(dp, tp_peer(k)), device_id_type=MESH,
        )

    def b_copy(k, who):
        return dp_copy(b_ref, b_all.at[pl.ds(who * held, held)], bdp_s, bdp_r, k)

    def a_copy(k, who):
        return dp_copy(a_ref, a_all.at[pl.ds(who * held, held)], adp_s, adp_r, k)

    for k in range(1, nd):
        b_copy(k, dp).start()
    for k in range(1, nd):
        a_copy(k, dp).start()

    def block_of(index):
        return lax.div(index * rows, block)

    own[1].wait()
    for k in range(1, nd):
        b_copy(k, dp_from(k)).wait_recv()
    for b in range(blocks):
        b_sel[b] = b_all[tab[dp, b]]
    b_in[j] = b_sel[block_of(j)]

    def bs_copy(k, who, whose):
        return tp_copy(b_sel.at[block_of(whose)], b_in.at[who], bs_s, bs_r, k)

    for k in range(1, ntp):
        bs_copy(k, j, tp_peer(k)).start()
    send_own(half, chunks)

    own[0].wait()
    for k in range(chunks):
        sib_copy(0, 0, k, 1 - c).wait_recv()

    def product(first, size, n):
        return dot_nt(g_all[pl.ds(first, size), :], w_v[slab(n, tile), :])

    def finish(zb, b, n, value):
        cols = slab(n, tile) if tiles > 1 else pl.ds(0, tile)
        filled = live[dp, b]
        keep = (lax.broadcasted_iota(jnp.int32, (block, 1), 0) < filled).astype(F32)
        extra = dot_nn(lo_t[b], a_sel[b, :, cols])
        hg_v[slab(b, block), cols] = (value * keep + adapter_scale * extra).astype(BF16)

    def mm_tiles(zb, lo, hi, final, wait_w):
        def one(n, carry):
            if wait_w:
                w_cp(n).wait()
            first = pl.multiple_of(zb * pair, pair)
            value = product(first, pair, n)
            if final:
                finish(zb, zb, n, value)
            else:
                cols = slab(n, tile) if tiles > 1 else pl.ds(0, tile)
                acc[pl.ds(first, pair), cols] = value
            return carry
        lax.fori_loop(lo, hi, one, 0)

    def fin_tiles(b):
        def one(n, carry):
            cols = slab(n, tile) if tiles > 1 else pl.ds(0, tile)
            finish(b, b, n, acc[slab(b, block), cols])
            return carry
        lax.fori_loop(0, tiles, one, 0)

    def hg_out(zb):
        return pltpu.make_async_copy(
            hg_v.at[slab(zb, block)], hg_ref.at[slab(zb, block)], out_sem.at[2 + zb]
        )

    def step(d, final, start=0, stop=chunks):
        def one(k, carry):
            if d + 1 < nz:
                receive(d + 1, k)
            lo, hi = lax.div(tiles * k, chunks), lax.div(tiles * (k + 1), chunks)
            for way in (0, 1) if d else (0,):
                @pl.when(has(way, d))
                def _():
                    mm_tiles(source(way, d), lo, hi, final, d == 0)
            return carry
        if start < stop:
            lax.fori_loop(start, stop, one, 0)
        if final and stop == chunks:
            for way in (0, 1) if d else (0,):
                @pl.when(has(way, d))
                def _():
                    hg_out(source(way, d)).start()

    def siblings(d):
        for way in (0, 1):
            @pl.when(has(way, d))
            def _():
                for k in range(chunks):
                    sib_copy(way, d, k, 1 - c).wait_recv()

    step(0, False, 0, half)

    for k in range(1, ntp):
        bs_copy(k, tp_from(k), j).wait_recv()
    low = jnp.zeros((rank, rows), F32)
    for s in range(ntp):
        low = low + dot_nt(b_in[s], g_all[slab(j, rows), s * feat : (s + 1) * feat])
    offset = lax.rem(j * rows, block)
    live_here = lax.broadcasted_iota(jnp.int32, (rank, rows), 1) + offset < live[dp, block_of(j)]
    low = (low * live_here.astype(F32)).astype(BF16)
    place = (
        lax.broadcasted_iota(jnp.int32, (rows, block), 1)
        == lax.broadcasted_iota(jnp.int32, (rows, block), 0) + offset
    ).astype(F32).astype(BF16)
    lo_all[j] = dot_nn(low, place).astype(BF16)

    def lo_copy(k, who):
        return tp_copy(lo_all.at[who], lo_all.at[who], lo_s, lo_r, k)

    for k in range(1, ntp):
        lo_copy(k, j).start()

    step(0, False, half)

    own[2].wait()
    for k in range(1, ntp):
        lo_copy(k, tp_from(k)).wait_recv()
    per_block = block // rows
    for b in range(blocks):
        value = lo_all[b * per_block].astype(F32)
        for s in range(1, per_block):
            value = value + lo_all[b * per_block + s].astype(F32)
        lo_bf[b] = value.astype(BF16)
        lo_t[b] = value.T.astype(BF16)
        ga[dp, b * rank : (b + 1) * rank, :] = (
            adapter_scale * dot_nn(lo_bf[b], h_v[b * block : (b + 1) * block, :])
        ).astype(BF16)

    def ga_copy(k, who):
        return dp_copy(ga.at[who], ga.at[who], ga_s, ga_r, k)

    def gb_copy(k, who):
        return dp_copy(gb.at[who], gb.at[who], gb_s, gb_r, k)

    for k in range(1, nd):
        ga_copy(k, dp).start()

    siblings(1)
    step(1, False, 0, half)

    own[3].wait()
    for k in range(1, nd):
        a_copy(k, dp_from(k)).wait_recv()
    for b in range(blocks):
        a_sel[b] = a_all[tab[dp, b]]
        value = dot_nt(a_sel[b], h_v[b * block : (b + 1) * block, :])
        for i in range(rank // piece):
            li_part[b * (rank // piece) + i] = value[i * piece : (i + 1) * piece, :]
    li_rs[j] = li_part[j]

    def rs_copy(k, who, whose):
        return tp_copy(li_part.at[whose], li_rs.at[who], rs_s, rs_r, k)

    for k in range(1, ntp):
        rs_copy(k, j, tp_peer(k)).start()

    step(1, False, half)

    for k in range(1, ntp):
        rs_copy(k, tp_from(k), j).wait_recv()
    total = li_rs[0]
    for s in range(1, ntp):
        total = total + li_rs[s]
    li_all[j] = total

    def li_copy(k, who):
        return tp_copy(li_all.at[who], li_all.at[who], li_s, li_r, k)

    for k in range(1, ntp):
        li_copy(k, j).start()

    if fused:
        for d in (0, 1):
            for way in (0, 1) if d else (0,):
                @pl.when(has(way, d))
                def _():
                    fin_tiles(source(way, d))
                    hg_out(source(way, d)).start()

    siblings(2)
    step(2, fused, 0, half)

    for k in range(1, ntp):
        li_copy(k, tp_from(k)).wait_recv()
    group = rank // piece
    for b in range(blocks):
        value = jnp.concatenate([li_all[b * group + i] for i in range(group)], axis=0)
        keep = lax.broadcasted_iota(jnp.int32, (rank, block), 1) < live[dp, b]
        li_bf[b] = (value * keep.astype(F32)).astype(BF16)

    def gb_block(b):
        gb[dp, slab(b, rank), :] = (
            adapter_scale * dot_nn(li_bf[b], g_all[slab(b, block), slab(j, feat)])
        ).astype(BF16)

    def gb_blocks(d):
        for way in (0, 1) if d else (0,):
            @pl.when(has(way, d))
            def _():
                gb_block(source(way, d))

    if fused:
        for d in range(nz - 1):
            gb_blocks(d)

    def chooser(g):
        r = lax.broadcasted_iota(jnp.int32, (held * rank, blocks * rank), 0)
        q = lax.broadcasted_iota(jnp.int32, (held * rank, blocks * rank), 1)
        same = (r & (rank - 1)) == (q & (rank - 1))
        which = jnp.zeros_like(q)
        for b in range(blocks):
            lane = (q >= b * rank) & (q < (b + 1) * rank)
            which = jnp.where(lane, tab[g, b] - dp * held, which)
        hit = (r >= which * rank) & (r < (which + 1) * rank) & same
        return hit.astype(F32).astype(BF16)

    picks = [chooser(g) for g in range(nd)]
    for k in range(1, nd):
        ga_copy(k, dp_from(k)).wait_recv()
    total = dot_nn(picks[0], ga[0])
    for g in range(1, nd):
        total = total + dot_nn(picks[g], ga[g])
    oa_v[...] = total.reshape(held, rank, ff)
    oa_cp = pltpu.make_async_copy(oa_v, oa_ref, out_sem.at[0])
    oa_cp.start()
    step(2, fused, half)
    for d in range(3, nz - 1):
        siblings(d)
        step(d, fused)

    siblings(nz - 1)
    if fused:
        gb_blocks(nz - 1)
    else:
        for b in range(blocks):
            gb_block(b)
    for k in range(1, nd):
        gb_copy(k, dp).start()

    step(nz - 1, fused)
    if not fused:
        for b in range(blocks):
            fin_tiles(b)
            hg_out(b).start()

    for k in range(1, nd):
        gb_copy(k, dp_from(k)).wait_recv()
    total = dot_nn(picks[0], gb[0])
    for g in range(1, nd):
        total = total + dot_nn(picks[g], gb[g])
    ob_v[...] = total.reshape(held, rank, feat)
    ob_cp = pltpu.make_async_copy(ob_v, ob_ref, out_sem.at[1])
    ob_cp.start()

    for d in range(nz):
        for way in (0, 1):
            if d < nz - 1:
                @pl.when(has(way, d) & has(1 - way, 1))
                def _():
                    for k in range(chunks):
                        nb_copy(way, d, k).wait_send()
            if d or way == 0:
                @pl.when(has(way, d))
                def _():
                    for k in range(chunks):
                        sib_copy(way, d, k, c).wait_send()
    for k in range(1, nd):
        for copy in (b_copy, a_copy, ga_copy, gb_copy):
            copy(k, dp).wait_send()
    for k in range(1, ntp):
        bs_copy(k, j, tp_peer(k)).wait_send()
        rs_copy(k, j, tp_peer(k)).wait_send()
        lo_copy(k, j).wait_send()
        li_copy(k, j).wait_send()
    for b in range(blocks):
        hg_out(b).wait()
    oa_cp.wait()
    ob_cp.wait()


def copy_kernel(blocks, hg, oa, ob, hg_out, oa_out, ob_out, hg_v, oa_v, ob_v, in_sem, out_sem):
    size = hg.shape[0] // blocks
    stages = [
        tuple(ref.at[pl.ds(b * size, size)] for ref in (hg, hg_v, hg_out)) for b in range(blocks)
    ] + [(oa, oa_v, oa_out), (ob, ob_v, ob_out)]
    loads = [pltpu.make_async_copy(s, v, in_sem.at[i]) for i, (s, v, _) in enumerate(stages)]
    stores = [pltpu.make_async_copy(v, o, out_sem.at[i]) for i, (_, v, o) in enumerate(stages)]
    for load in loads:
        load.start()
    for load, store in zip(loads, stores):
        load.wait()
        store.start()
    for store in stores:
        store.wait()


def shards(nd, ntp, g, h, w, a, bm, tab, live):
    blocks = tab.shape[1]
    group_rows, ff = h.shape
    block = group_rows // blocks
    held, rank, _ = a.shape
    feat = bm.shape[2]
    rows, width = g.shape
    nz = ntp // 2
    chunks = max(1, min(2, rows // 16))
    tiles = ff // 256 if ff % 256 == 0 else 1
    piece = blocks * rank // ntp
    V = pltpu.VMEM
    dma = lambda *s: pltpu.SemaphoreType.DMA(s)
    scratch = [
        V((group_rows, width), BF16), V((group_rows, ff), BF16), V((ff, width), BF16),
        V((nd * held, rank, ff), BF16), V((nd * held, rank, feat), BF16),
        V((blocks, rank, ff), BF16), V((blocks, rank, feat), BF16),
        V((ntp, rank, feat), BF16), V((ntp, rank, block), BF16),
        V((blocks, rank, block), BF16), V((blocks, block, rank), BF16),
        V((ntp, piece, block), F32), V((ntp, piece, block), F32), V((ntp, piece, block), F32),
        V((blocks, rank, block), BF16),
        V((nd, blocks * rank, ff), BF16), V((nd, blocks * rank, feat), BF16),
        V((group_rows, ff), F32), V((group_rows, ff), BF16),
        V((held, rank, ff), F32), V((held, rank, feat), F32),
        dma(tiles), dma(4), dma(2 + blocks),
        dma(2, nz, chunks), dma(2, nz + 1, chunks), dma(2, nz, chunks), dma(2, nz, chunks),
        dma(nd), dma(nd), dma(nd), dma(nd), dma(ntp), dma(ntp),
        dma(ntp), dma(ntp), dma(ntp), dma(ntp), dma(ntp), dma(ntp),
        dma(nd), dma(nd), dma(nd), dma(nd),
    ]
    any_spec = pl.BlockSpec(memory_space=pl.ANY)
    smem = pl.BlockSpec(memory_space=pltpu.SMEM)
    hg, oa, ob = pl.pallas_call(
        functools.partial(
            kernel, nd, ntp, blocks, block, rank, held, rows, chunks, ff, feat, tiles
        ),
        out_shape=(
            jax.ShapeDtypeStruct((group_rows, ff), BF16),
            jax.ShapeDtypeStruct((held, rank, ff), F32),
            jax.ShapeDtypeStruct((held, rank, feat), F32),
        ),
        in_specs=[any_spec] * 5 + [smem] * 2,
        out_specs=(any_spec,) * 3,
        scratch_shapes=scratch,
        compiler_params=pltpu.CompilerParams(
            collective_id=0, has_side_effects=True, vmem_limit_bytes=62 * 1024 * 1024
        ),
    )(g, h, w, a, bm, tab, live)
    results = (hg, oa, ob)
    return pl.pallas_call(
        functools.partial(copy_kernel, blocks),
        out_shape=tuple(jax.ShapeDtypeStruct(x.shape, x.dtype) for x in results),
        in_specs=[any_spec] * 3,
        out_specs=(any_spec,) * 3,
        scratch_shapes=[V(x.shape, x.dtype) for x in results] + [dma(blocks + 2), dma(blocks + 2)],
        compiler_params=pltpu.CompilerParams(vmem_limit_bytes=62 * 1024 * 1024),
    )(*results)


def far_start(z, nz, start, size, width):
    return jnp.where(z < nz // 2, start, width - start - size)


def line_kernel(
    nd, nz, blocks, block, rank, held, rows, sizes, ff, feat, width,
    g_ref, h_ref, w_ref, a_ref, b_ref, tab, live,
    hg_v, oa_v, ob_v, g_all, w_v, acc, keep_v,
    h_v, a_own, b_own, a_out, b_out, a_in, b_from, a_sel, b_sel, b_in,
    lo_part, lo_all, lo_t, li_part, li_sib, li_sum, li_rs, li_all, ga, gb,
    w_sem, own_sem, relay,
    nb_s, nb_r, sib_s, sib_r, row_s, row_r, bdp_s, bdp_r, adp_s, adp_r,
    bs_s, bs_r, lo_s, lo_r, rs_s, rs_r, ag_s, ag_r, pair_s, pair_r,
    ga_s, ga_r, gb_s, gb_r,
):
    dp = lax.axis_index("dp")
    j = lax.axis_index("seqtp")
    z = lax.div(j, 2)
    c = lax.rem(j, 2)
    sib = z * 2 + 1 - c
    chunks = len(sizes)
    tile = 256
    tiles = ff // tile
    piece = blocks * rank // (2 * nz)
    pair_rows = 2 * block
    near = lax.div(z, 2)
    far = 1 - near
    starts = [sum(sizes[:i]) for i in range(chunks)]

    def slab(index, size):
        return pl.ds(pl.multiple_of(index * size, size), size)

    def has(way, d):
        return z >= d if way == 0 else z + d < nz

    def source(way, d):
        return z - d if way == 0 else z + d

    def dp_peer(k):
        return lax.rem(dp + k, nd)

    def dp_from(k):
        return lax.rem(dp + nd - k, nd)

    def z_peer(k):
        return lax.rem(z + k, nz)

    def z_from(k):
        return lax.rem(z + nz - k, nz)

    def toward(way):
        return (dp, j + 2 if way == 0 else j - 2)

    barrier = pltpu.get_barrier_semaphore()
    for way in (0, 1):
        @pl.when(has(1 - way, 1))
        def _():
            pl.semaphore_signal(barrier, inc=1, device_id=toward(way), device_id_type=MESH)
    pl.semaphore_signal(barrier, inc=1, device_id=(dp, sib), device_id_type=MESH)
    for k in range(1, nd):
        pl.semaphore_signal(barrier, inc=1, device_id=(dp_peer(k), j), device_id_type=MESH)

    own = [
        pltpu.make_async_copy(b_ref, b_own, own_sem.at[0]),
        pltpu.make_async_copy(g_ref, g_all.at[slab(j, rows)], own_sem.at[1]),
        pltpu.make_async_copy(h_ref, h_v, own_sem.at[2]),
        pltpu.make_async_copy(a_ref, a_own, own_sem.at[3]),
    ]
    w_cp = [
        pltpu.make_async_copy(w_ref.at[pl.ds(n * tile, tile)], w_v.at[pl.ds(n * tile, tile)], w_sem.at[n])
        for n in range(tiles)
    ]
    own[0].start()
    own[3].start()
    own[1].start()

    @pl.when(has(0, 1) & has(1, 1))
    def _():
        pl.semaphore_wait(barrier, nd + 2)

    @pl.when(jnp.logical_not(has(0, 1) & has(1, 1)))
    def _():
        pl.semaphore_wait(barrier, nd + 1)

    def part(ref, first, way, i):
        start = starts[i] if way == 1 else width - starts[i] - sizes[i]
        return ref.at[slab(first, rows), pl.ds(start, sizes[i])]

    def nb_copy(way, d, i):
        first = source(way, d) * 2 + c
        src = part(g_ref, 0, way, i) if d == 0 else part(g_all, first, way, i)
        return pltpu.make_async_remote_copy(
            src_ref=src, dst_ref=part(g_all, first, way, i),
            send_sem=nb_s.at[way, d, i], recv_sem=nb_r.at[way, d + 1, i],
            device_id=toward(way), device_id_type=MESH,
        )

    def nb_arrival(way, d, i):
        here = part(g_all, source(way, d) * 2 + c, way, i)
        return pltpu.make_async_remote_copy(
            src_ref=here, dst_ref=here,
            send_sem=nb_s.at[way, d - 1, i], recv_sem=nb_r.at[way, d, i],
            device_id=(dp, sib), device_id_type=MESH,
        )

    def sib_copy(way, d, i, core):
        here = part(g_all, source(way, d) * 2 + core, way, i)
        return pltpu.make_async_remote_copy(
            src_ref=here, dst_ref=here,
            send_sem=sib_s.at[way, d, i], recv_sem=sib_r.at[way, d, i],
            device_id=(dp, sib), device_id_type=MESH,
        )

    def row_copy(index):
        return pltpu.make_async_remote_copy(
            src_ref=g_ref, dst_ref=g_all.at[slab(index, rows)],
            send_sem=row_s, recv_sem=row_r, device_id=(dp, sib), device_id_type=MESH,
        )

    def onward(way, d):
        return has(way, d) & has(1 - way, 1)

    def advance(n):
        d, i = n // chunks, n % chunks
        if d < nz - 1:
            for way in (0, 1):
                @pl.when(onward(way, d))
                def _():
                    nb_copy(way, d, i).start()

    def event(n):
        d, i = n // chunks, n % chunks
        for way in (0, 1):
            @pl.when(has(way, d + 1))
            def _():
                nb_arrival(way, d + 1, i).wait_recv()
                sib_copy(way, d + 1, i, c).start()
        for way in (0, 1):
            @pl.when(onward(way, d))
            def _():
                nb_copy(way, d, i).wait_send()

    def landed(n):
        d, i = n // chunks + 1, n % chunks
        for way in (0, 1):
            @pl.when(has(way, d))
            def _():
                sib_copy(way, d, i, 1 - c).wait_recv()

    def dp_copy(src, dst, s, r, k):
        return pltpu.make_async_remote_copy(
            src_ref=src, dst_ref=dst, send_sem=s.at[k], recv_sem=r.at[k],
            device_id=(dp_peer(k), j), device_id_type=MESH,
        )

    def z_copy(src, dst, s, r, k):
        return pltpu.make_async_remote_copy(
            src_ref=src, dst_ref=dst, send_sem=s.at[k], recv_sem=r.at[k],
            device_id=(dp, z_peer(k) * 2 + c), device_id_type=MESH,
        )

    def core_copy(src, dst, k):
        return pltpu.make_async_remote_copy(
            src_ref=src, dst_ref=dst, send_sem=pair_s.at[k], recv_sem=pair_r.at[k],
            device_id=(dp, sib), device_id_type=MESH,
        )

    def b_copy(k, who):
        return dp_copy(b_out.at[k], b_from.at[who], bdp_s, bdp_r, k)

    def a_copy(k, who):
        return dp_copy(a_out.at[k], a_in.at[who], adp_s, adp_r, k)

    def at_owner(group, b):
        return jnp.clip(tab[group, b] - dp * held, 0, held - 1)

    def bs_copy(k, who, whose):
        return z_copy(b_sel.at[whose], b_in.at[who], bs_s, bs_r, k)

    def lo_copy(k, who):
        return z_copy(lo_all.at[who], lo_all.at[who], lo_s, lo_r, k)

    def rs_copy(k, who, whose):
        return z_copy(li_sum.at[whose], li_rs.at[who], rs_s, rs_r, k)

    def ag_copy(k, who):
        return z_copy(li_all.at[c * nz + who], li_all.at[c * nz + who], ag_s, ag_r, k)

    def ga_copy(k, who):
        return dp_copy(ga.at[who], ga.at[who], ga_s, ga_r, k)

    def gb_copy(k, who):
        return dp_copy(gb.at[who], gb.at[who], gb_s, gb_r, k)

    def lo_pair(core):
        return core_copy(lo_part.at[core], lo_part.at[core], 0)

    def li_pair(core):
        return core_copy(li_part.at[1 - core], li_sib, 1)

    def ag_pair(core):
        here = li_all.at[pl.ds(core * nz, nz)]
        return core_copy(here, here, 2)

    advance(0)
    advance(1)
    advance(2)
    row_copy(j).start()
    own[0].wait()
    for k in range(1, nd):
        for b in range(blocks):
            b_out[k, b] = b_own[at_owner(dp_peer(k), b)]
        b_copy(k, dp).start()
    for b in range(blocks):
        b_from[dp, b] = b_own[at_owner(dp, b)]
    for way in (0, 1):
        @pl.when(has(way, 1) & has(1 - way, 1))
        def _():
            pl.semaphore_signal(relay.at[way, 2], inc=1, device_id=toward(way), device_id_type=MESH)
    own[2].start()
    for n in range(tiles):
        w_cp[n].start()
    own[3].wait()
    for k in range(1, nd):
        for b in range(blocks):
            a_out[k, b] = a_own[at_owner(dp_peer(k), b)]
        a_copy(k, dp).start()
    for b in range(blocks):
        a_in[dp, b] = a_own[at_owner(dp, b)]

    for d in range(2, nz):
        for way in (0, 1):
            @pl.when(has(way, d))
            def _():
                pl.semaphore_wait(relay.at[way, d], 1)
                if d + 1 < nz:
                    @pl.when(has(1 - way, 1))
                    def _():
                        pl.semaphore_signal(
                            relay.at[way, d + 1], inc=1, device_id=toward(way), device_id_type=MESH
                        )

    for k in range(1, nd):
        b_copy(k, dp_from(k)).wait_recv()
    for b in range(blocks):
        b_sel[b] = b_from[lax.div(tab[dp, b], held), b]
    b_in[z] = b_sel[z]
    for k in range(1, nz):
        bs_copy(k, z, z_peer(k)).start()

    event(0)
    advance(3)
    event(1)
    advance(4)

    own[1].wait()
    row_copy(sib).wait_recv()
    for k in range(1, nz):
        bs_copy(k, z_from(k), z).wait_recv()
    low = jnp.zeros((rank, block), F32)
    for s in range(nz):
        low = low + dot_nt(b_in[s], g_all[slab(z, block), slab(2 * s + c, feat)])
    lo_part[c] = low
    lo_pair(c).start()

    event(2)

    lo_pair(1 - c).wait_recv()
    lanes = lax.broadcasted_iota(jnp.int32, (rank, block), 1)
    low = lo_part[0] + lo_part[1]
    lo_all[z] = (low * (lanes < live[dp, z]).astype(F32)).astype(BF16)
    for k in range(1, nz):
        lo_copy(k, z).start()
    advance(5)

    event(3)
    advance(6)
    event(4)

    for k in range(1, nd):
        a_copy(k, dp_from(k)).wait_recv()
    own[2].wait()
    for b in range(blocks):
        a_sel[b] = a_in[lax.div(tab[dp, b], held), b]
        value = dot_nt(a_sel[b], h_v[b * block : (b + 1) * block, :])
        for i in range(rank // piece):
            at = b * (rank // piece) + i
            li_part[at // nz, at % nz] = value[i * piece : (i + 1) * piece, :]
    li_pair(c).start()
    for k in range(1, nz):
        lo_copy(k, z_from(k)).wait_recv()
    for b in range(blocks):
        lo_t[b] = lo_all[b].astype(F32).T.astype(BF16)
        ga[dp, b * rank : (b + 1) * rank, :] = (
            adapter_scale * dot_nn(lo_all[b], h_v[b * block : (b + 1) * block, :])
        ).astype(BF16)
    for k in range(1, nd):
        ga_copy(k, dp).start()
    li_pair(1 - c).wait_recv()
    li_sum[...] = li_part[c] + li_sib[...]
    li_rs[z] = li_sum[z]
    for k in range(1, nz):
        rs_copy(k, z, z_peer(k)).start()
    advance(7)

    def keep_of(b):
        return (lax.broadcasted_iota(jnp.int32, (block, 1), 0) < live[dp, b]).astype(F32)

    for n in range(chunks):
        landed(n)
    for n in range(tiles):
        w_cp[n].wait()

    def near_tiles(lo, hi):
        def one(n, carry):
            cols = slab(n, tile)
            value = dot_nt(g_all[slab(near, pair_rows), :], w_v[slab(n, tile), :])
            for s in range(2):
                b = near * 2 + s
                extra = dot_nn(lo_t[b], a_sel[b, :, cols])
                total = value[s * block : (s + 1) * block] + adapter_scale * extra
                hg_v[s * block : (s + 1) * block, cols] = (total * keep_of(b)).astype(BF16)
            return carry
        lax.fori_loop(lo, hi, one, 0)

    near_tiles(0, 1)
    event(5)
    advance(8)
    near_tiles(1, 3)
    event(6)
    near_tiles(3, 4)

    for k in range(1, nz):
        rs_copy(k, z_from(k), z).wait_recv()
    total = li_rs[0]
    for s in range(1, nz):
        total = total + li_rs[s]
    whole = c * nz + z
    lanes = lax.broadcasted_iota(jnp.int32, (piece, block), 1)
    filled = live[dp, lax.div(whole * piece, rank)]
    li_all[whole] = (total * (lanes < filled).astype(F32)).astype(BF16)
    for k in range(1, nz):
        ag_copy(k, z).start()
    advance(9)

    near_tiles(4, 5)
    event(7)
    advance(10)
    near_tiles(5, tiles)

    def gb_block(b):
        group = rank // piece
        rows_of = jnp.concatenate(
            [li_all[b * group + i].astype(F32) for i in range(group)], axis=0
        ).astype(BF16)
        gb[dp, slab(b, rank), :] = (
            adapter_scale * dot_nn(rows_of, g_all[slab(b, block), slab(j, feat)])
        ).astype(BF16)

    def chooser(g):
        r = lax.broadcasted_iota(jnp.int32, (held * rank, blocks * rank), 0)
        q = lax.broadcasted_iota(jnp.int32, (held * rank, blocks * rank), 1)
        same = (r & (rank - 1)) == (q & (rank - 1))
        which = jnp.zeros_like(q)
        for b in range(blocks):
            lane = (q >= b * rank) & (q < (b + 1) * rank)
            which = jnp.where(lane, tab[g, b] - dp * held, which)
        hit = (r >= which * rank) & (r < (which + 1) * rank) & same
        return hit.astype(F32).astype(BF16)

    def owned(ref):
        total = dot_nn(chooser(0), ref[0])
        for g in range(1, nd):
            total = total + dot_nn(chooser(g), ref[g])
        return total


    for s in range(2):
        b = far * 2 + s
        acc[s * block : (s + 1) * block, :] = adapter_scale * dot_nn(lo_t[b], a_sel[b])
        keep_v[s * block : (s + 1) * block, :] = jnp.broadcast_to(keep_of(b), (block, 128))

    def drain(d, stop=chunks, first=0):
        for way in (0, 1):
            for i in range(first, stop):
                if d:
                    @pl.when(has(way, d))
                    def _():
                        sib_copy(way, d, i, c).wait_send()

    row_copy(j).wait_send()
    drain(1)
    for k in range(1, nd):
        for copy in (b_copy, a_copy):
            copy(k, dp).wait_send()
    for k in range(1, nz):
        bs_copy(k, z, z_peer(k)).wait_send()
        lo_copy(k, z).wait_send()
        rs_copy(k, z, z_peer(k)).wait_send()
    for copy in (lo_pair, li_pair):
        copy(c).wait_send()
    for n in range(chunks, 2 * chunks):
        landed(n)

    def far_chunk(i):
        start = far_start(z, nz, starts[i], sizes[i], width)
        deep = pl.ds(pl.multiple_of(start, 128), sizes[i])
        for n in range(tiles):
            cols = pl.ds(n * tile, tile)
            acc[:, cols] += dot_nt(g_all[slab(far, pair_rows), deep], w_v[cols, deep])

    for i in range(chunks):
        event(2 * chunks + i)
        advance(2 * chunks + i + 3)
        landed(2 * chunks + i)
        if i == 0:
            for k in range(1, nz):
                ag_copy(k, z_from(k)).wait_recv()
            ag_pair(c).start()
        if i < chunks - 1:
            far_chunk(i)
        if i == 0:
            ag_pair(1 - c).wait_recv()
            for b in range(blocks):
                gb_block(b)
            for k in range(1, nd):
                gb_copy(k, dp).start()
        if i == 1:
            for k in range(1, nd):
                ga_copy(k, dp_from(k)).wait_recv()
            oa_v[...] = owned(ga).reshape(held, rank, ff)
        if i == chunks - 2:
            for k in range(1, nd):
                gb_copy(k, dp_from(k)).wait_recv()
            ob_v[...] = owned(gb).reshape(held, rank, feat)
            for k in range(1, nd):
                gb_copy(k, dp).wait_send()
                ga_copy(k, dp).wait_send()
            for k in range(1, nz):
                ag_copy(k, z).wait_send()
            ag_pair(c).wait_send()
            drain(2)
            for d in range(3, nz):
                drain(d, chunks - 1)
    for d in range(3, nz):
        drain(d, chunks, chunks - 1)


def last_kernel(
    nz, size, hg, oa, ob, g_all, w_v, acc, keep_v, hg_out, oa_out, ob_out, far_v, sem, tile_sem
):
    z = lax.div(lax.axis_index("seqtp"), 2)
    near = lax.div(z, 2)
    pair_rows, ff = hg.shape
    width = w_v.shape[1]
    tile = 256
    near_rows = pl.ds(pl.multiple_of(near * pair_rows, pair_rows), pair_rows)
    far_rows = pl.ds(pl.multiple_of((1 - near) * pair_rows, pair_rows), pair_rows)
    copies = [(hg, hg_out.at[near_rows]), (oa, oa_out), (ob, ob_out)]
    copies = [pltpu.make_async_copy(s, o, sem.at[i]) for i, (s, o) in enumerate(copies)]
    for copy in copies:
        copy.start()
    start = far_start(z, nz, width - size, size, width)
    deep = pl.ds(pl.multiple_of(start, 128), size)
    keep = keep_v[:, :1]
    for n in range(ff // tile):
        cols = pl.ds(n * tile, tile)
        value = acc[:, cols] + dot_nt(g_all[far_rows, deep], w_v[cols, deep])
        far_v[:, cols] = (value * keep).astype(BF16)
        copies.append(
            pltpu.make_async_copy(far_v.at[:, cols], hg_out.at[far_rows, cols], tile_sem.at[n])
        )
        copies[-1].start()
    for copy in copies:
        copy.wait()


def line_shards(nd, ntp, g, h, w, a, bm, tab, live):
    blocks = tab.shape[1]
    group_rows, ff = h.shape
    block = group_rows // blocks
    held, rank, _ = a.shape
    feat = bm.shape[2]
    rows, width = g.shape
    nz = ntp // 2
    sizes = (width // 4,) * 4
    tiles = ff // 256
    chunks = len(sizes)
    piece = blocks * rank // ntp
    V = pltpu.VMEM
    dma = lambda *s: pltpu.SemaphoreType.DMA(s)
    scratch = [
        V((group_rows, ff), BF16), V((held, rank, ff), BF16), V((held, rank, feat), BF16),
        V((nd, blocks, rank, ff), BF16), V((nd, blocks, rank, feat), BF16),
        V((nd, blocks, rank, ff), BF16), V((nd, blocks, rank, feat), BF16),
        V((blocks, rank, ff), BF16), V((blocks, rank, feat), BF16), V((nz, rank, feat), BF16),
        V((2, rank, block), F32), V((blocks, rank, block), BF16), V((blocks, block, rank), BF16),
        V((2, nz, piece, block), F32), V((nz, piece, block), F32), V((nz, piece, block), F32),
        V((nz, piece, block), F32), V((ntp, piece, block), BF16),
        V((nd, blocks * rank, ff), BF16), V((nd, blocks * rank, feat), BF16),
        dma(tiles), dma(4), pltpu.SemaphoreType.REGULAR((2, nz)),
        dma(2, nz, chunks), dma(2, nz + 1, chunks), dma(2, nz, chunks), dma(2, nz, chunks),
        pltpu.SemaphoreType.DMA, pltpu.SemaphoreType.DMA,
        dma(nd), dma(nd), dma(nd), dma(nd),
        dma(nz), dma(nz), dma(nz), dma(nz), dma(nz), dma(nz), dma(nz), dma(nz), dma(3), dma(3),
        dma(nd), dma(nd), dma(nd), dma(nd),
    ]
    hbm = pl.BlockSpec(memory_space=pltpu.HBM)
    smem = pl.BlockSpec(memory_space=pltpu.SMEM)
    vmem = pl.BlockSpec(memory_space=pltpu.VMEM)
    results = pl.pallas_call(
        functools.partial(
            line_kernel, nd, nz, blocks, block, rank, held, rows, sizes, ff, feat, width
        ),
        out_shape=(
            V((2 * block, ff), BF16), V((held, rank, ff), F32), V((held, rank, feat), F32),
            V((group_rows, width), BF16), V((ff, width), BF16), V((2 * block, ff), F32),
            V((2 * block, 128), F32),
        ),
        in_specs=[hbm] * 5 + [smem] * 2,
        out_specs=(vmem,) * 7,
        scratch_shapes=scratch,
        compiler_params=pltpu.CompilerParams(
            collective_id=1, has_side_effects=True, vmem_limit_bytes=41 * 1024 * 1024
        ),
    )(g, h, w, a, bm, tab, live)
    return pl.pallas_call(
        functools.partial(last_kernel, nz, sizes[-1]),
        out_shape=(
            jax.ShapeDtypeStruct((group_rows, ff), BF16),
            jax.ShapeDtypeStruct((held, rank, ff), F32),
            jax.ShapeDtypeStruct((held, rank, feat), F32),
        ),
        in_specs=[vmem] * 7,
        out_specs=(hbm,) * 3,
        scratch_shapes=[V((2 * block, ff), BF16), dma(3), dma(tiles)],
        compiler_params=pltpu.CompilerParams(vmem_limit_bytes=8 * 1024 * 1024),
    )(*results)


def body(nd, ntp, g, h, w, a, bm, tab, live):
    blocks = tab.shape[1]
    group_rows, ff = h.shape
    rows, width = g.shape
    line = (
        ntp == 8 and blocks == 4 and 8 * rows == group_rows and ff % 256 == 0
        and width == ntp * bm.shape[2] and bm.shape[2] % 128 == 0
        and blocks * a.shape[1] == 8 * ntp
    )
    return (line_shards if line else shards)(nd, ntp, g, h, w, a, bm, tab, live)


def solution(mesh):
    in_specs = (
        P(("dp", "seqtp"), None),
        P("dp", "seqtp"),
        P("seqtp", None),
        P("dp", None, "seqtp"),
        P("dp", None, "seqtp"),
        P(),
        P(),
    )
    out_specs = (P("dp", "seqtp"), P("dp", None, "seqtp"), P("dp", None, "seqtp"))
    step = functools.partial(body, mesh.shape["dp"], mesh.shape["seqtp"])
    return jax.shard_map(step, mesh=mesh, in_specs=in_specs, out_specs=out_specs, check_vma=False)
```

```python
import functools

import jax
import jax.numpy as jnp
from jax import lax
from jax.experimental import pallas as pl
from jax.experimental.pallas import tpu as pltpu
from jax.sharding import PartitionSpec as P

adapter_scale = 0.5
MESH = pl.DeviceIdType.MESH
F32 = jnp.float32
BF16 = jnp.bfloat16


def dot_nt(a, b):
    return lax.dot_general(a, b, (((1,), (1,)), ((), ())), preferred_element_type=F32)


def dot_nn(a, b):
    return lax.dot_general(a, b, (((1,), (0,)), ((), ())), preferred_element_type=F32)


def kernel(
    nd, ntp, blocks, block, rank, held, rows, chunks, ff, feat, tiles,
    g_ref, h_ref, w_ref, a_ref, b_ref, tab, live,
    hg_ref, oa_ref, ob_ref,
    g_all, h_v, w_v, a_all, b_all, a_sel, b_sel, b_in, lo_all, lo_bf, lo_t,
    li_part, li_rs, li_all, li_bf, ga, gb, acc, hg_v, oa_v, ob_v,
    w_sem, own_sem, out_sem,
    nb_s, nb_r, sib_s, sib_r, bdp_s, bdp_r, adp_s, adp_r, bs_s, bs_r,
    lo_s, lo_r, rs_s, rs_r, li_s, li_r, ga_s, ga_r, gb_s, gb_r,
):
    nz = ntp // 2
    dp = lax.axis_index("dp")
    j = lax.axis_index("seqtp")
    z = lax.div(j, 2)
    c = lax.rem(j, 2)
    sib = z * 2 + 1 - c
    crow = rows // chunks
    tile = ff // tiles
    pair = 2 * rows
    piece = blocks * rank // ntp
    fused = pair == block

    def dp_peer(k):
        return lax.rem(dp + k, nd)

    def tp_peer(k):
        return lax.rem(j + k, ntp)

    def dp_from(k):
        return lax.rem(dp + nd - k, nd)

    def tp_from(k):
        return lax.rem(j + ntp - k, ntp)

    def slab(index, size):
        return pl.ds(pl.multiple_of(index * size, size), size)

    w_cp = lambda n: pltpu.make_async_copy(
        w_ref.at[slab(n, tile)], w_v.at[slab(n, tile)], w_sem.at[n]
    )
    own = [
        pltpu.make_async_copy(g_ref, g_all.at[slab(j, rows)], own_sem.at[0]),
        pltpu.make_async_copy(b_ref, b_all.at[pl.ds(dp * held, held)], own_sem.at[1]),
        pltpu.make_async_copy(h_ref, h_v, own_sem.at[2]),
        pltpu.make_async_copy(a_ref, a_all.at[pl.ds(dp * held, held)], own_sem.at[3]),
    ]
    own[0].start()
    own[1].start()
    for n in range(tiles):
        w_cp(n).start()
    own[2].start()
    own[3].start()

    barrier = pltpu.get_barrier_semaphore()
    for k in range(1, nd):
        pl.semaphore_signal(barrier, inc=1, device_id=(dp_peer(k), j), device_id_type=MESH)
    for k in range(1, ntp):
        pl.semaphore_signal(barrier, inc=1, device_id=(dp, tp_peer(k)), device_id_type=MESH)
    pl.semaphore_wait(barrier, nd - 1 + ntp - 1)

    def source(way, d):
        return z - d if way == 0 else z + d

    def has(way, d):
        return z >= d if way == 0 else z + d < nz

    def chunk_at(ref, first, k):
        return ref.at[pl.ds(pl.multiple_of(first + k * crow, crow), crow)]

    def nb_copy(way, d, k):
        first = (source(way, d) * 2 + c) * rows
        src = chunk_at(g_ref, 0, k) if d == 0 else chunk_at(g_all, first, k)
        return pltpu.make_async_remote_copy(
            src_ref=src, dst_ref=chunk_at(g_all, first, k),
            send_sem=nb_s.at[way, d, k], recv_sem=nb_r.at[way, d + 1, k],
            device_id=(dp, j + 2 if way == 0 else j - 2), device_id_type=MESH,
        )

    def nb_arrival(way, d, k):
        first = (source(way, d) * 2 + c) * rows
        here = chunk_at(g_all, first, k)
        return pltpu.make_async_remote_copy(
            src_ref=here, dst_ref=here,
            send_sem=nb_s.at[way, d, k], recv_sem=nb_r.at[way, d, k],
            device_id=(dp, sib), device_id_type=MESH,
        )

    def sib_copy(way, d, k, core):
        first = (source(way, d) * 2 + core) * rows
        src = chunk_at(g_ref, 0, k) if d == 0 else chunk_at(g_all, first, k)
        return pltpu.make_async_remote_copy(
            src_ref=src, dst_ref=chunk_at(g_all, first, k),
            send_sem=sib_s.at[way, d, k], recv_sem=sib_r.at[way, d, k],
            device_id=(dp, sib), device_id_type=MESH,
        )

    def send_on(way, d, k):
        @pl.when(has(way, d) & has(1 - way, 1))
        def _():
            nb_copy(way, d, k).start()

    def receive(d, k):
        for way in (0, 1):
            @pl.when(has(way, d))
            def _():
                nb_arrival(way, d, k).wait_recv()
            if d < nz - 1:
                send_on(way, d, k)

            @pl.when(has(way, d))
            def _():
                sib_copy(way, d, k, c).start()

    half = chunks // 2

    def send_own(lo, hi):
        for k in range(lo, hi):
            send_on(0, 0, k)
            send_on(1, 0, k)
            sib_copy(0, 0, k, c).start()

    send_own(0, half)

    def dp_copy(src, dst, s, r, k):
        return pltpu.make_async_remote_copy(
            src_ref=src, dst_ref=dst, send_sem=s.at[k], recv_sem=r.at[k],
            device_id=(dp_peer(k), j), device_id_type=MESH,
        )

    def tp_copy(src, dst, s, r, k):
        return pltpu.make_async_remote_copy(
            src_ref=src, dst_ref=dst, send_sem=s.at[k], recv_sem=r.at[k],
            device_id=(dp, tp_peer(k)), device_id_type=MESH,
        )

    def b_copy(k, who):
        return dp_copy(b_ref, b_all.at[pl.ds(who * held, held)], bdp_s, bdp_r, k)

    def a_copy(k, who):
        return dp_copy(a_ref, a_all.at[pl.ds(who * held, held)], adp_s, adp_r, k)

    for k in range(1, nd):
        b_copy(k, dp).start()
    for k in range(1, nd):
        a_copy(k, dp).start()

    def block_of(index):
        return lax.div(index * rows, block)

    own[1].wait()
    for k in range(1, nd):
        b_copy(k, dp_from(k)).wait_recv()
    for b in range(blocks):
        b_sel[b] = b_all[tab[dp, b]]
    b_in[j] = b_sel[block_of(j)]

    def bs_copy(k, who, whose):
        return tp_copy(b_sel.at[block_of(whose)], b_in.at[who], bs_s, bs_r, k)

    for k in range(1, ntp):
        bs_copy(k, j, tp_peer(k)).start()
    send_own(half, chunks)

    own[0].wait()
    for k in range(chunks):
        sib_copy(0, 0, k, 1 - c).wait_recv()

    def product(first, size, n):
        return dot_nt(g_all[pl.ds(first, size), :], w_v[slab(n, tile), :])

    def finish(zb, b, n, value):
        cols = slab(n, tile) if tiles > 1 else pl.ds(0, tile)
        filled = live[dp, b]
        keep = (lax.broadcasted_iota(jnp.int32, (block, 1), 0) < filled).astype(F32)
        extra = dot_nn(lo_t[b], a_sel[b, :, cols])
        hg_v[slab(b, block), cols] = (value * keep + adapter_scale * extra).astype(BF16)

    def mm_tiles(zb, lo, hi, final, wait_w):
        def one(n, carry):
            if wait_w:
                w_cp(n).wait()
            first = pl.multiple_of(zb * pair, pair)
            value = product(first, pair, n)
            if final:
                finish(zb, zb, n, value)
            else:
                cols = slab(n, tile) if tiles > 1 else pl.ds(0, tile)
                acc[pl.ds(first, pair), cols] = value
            return carry
        lax.fori_loop(lo, hi, one, 0)

    def fin_tiles(b):
        def one(n, carry):
            cols = slab(n, tile) if tiles > 1 else pl.ds(0, tile)
            finish(b, b, n, acc[slab(b, block), cols])
            return carry
        lax.fori_loop(0, tiles, one, 0)

    def hg_out(zb):
        return pltpu.make_async_copy(
            hg_v.at[slab(zb, block)], hg_ref.at[slab(zb, block)], out_sem.at[2 + zb]
        )

    def step(d, final, start=0, stop=chunks):
        def one(k, carry):
            if d + 1 < nz:
                receive(d + 1, k)
            lo, hi = lax.div(tiles * k, chunks), lax.div(tiles * (k + 1), chunks)
            for way in (0, 1) if d else (0,):
                @pl.when(has(way, d))
                def _():
                    mm_tiles(source(way, d), lo, hi, final, d == 0)
            return carry
        if start < stop:
            lax.fori_loop(start, stop, one, 0)
        if final and stop == chunks:
            for way in (0, 1) if d else (0,):
                @pl.when(has(way, d))
                def _():
                    hg_out(source(way, d)).start()

    def siblings(d):
        for way in (0, 1):
            @pl.when(has(way, d))
            def _():
                for k in range(chunks):
                    sib_copy(way, d, k, 1 - c).wait_recv()

    step(0, False, 0, half)

    for k in range(1, ntp):
        bs_copy(k, tp_from(k), j).wait_recv()
    low = jnp.zeros((rank, rows), F32)
    for s in range(ntp):
        low = low + dot_nt(b_in[s], g_all[slab(j, rows), s * feat : (s + 1) * feat])
    offset = lax.rem(j * rows, block)
    live_here = lax.broadcasted_iota(jnp.int32, (rank, rows), 1) + offset < live[dp, block_of(j)]
    low = (low * live_here.astype(F32)).astype(BF16)
    place = (
        lax.broadcasted_iota(jnp.int32, (rows, block), 1)
        == lax.broadcasted_iota(jnp.int32, (rows, block), 0) + offset
    ).astype(F32).astype(BF16)
    lo_all[j] = dot_nn(low, place).astype(BF16)

    def lo_copy(k, who):
        return tp_copy(lo_all.at[who], lo_all.at[who], lo_s, lo_r, k)

    for k in range(1, ntp):
        lo_copy(k, j).start()

    step(0, False, half)

    own[2].wait()
    for k in range(1, ntp):
        lo_copy(k, tp_from(k)).wait_recv()
    per_block = block // rows
    for b in range(blocks):
        value = lo_all[b * per_block].astype(F32)
        for s in range(1, per_block):
            value = value + lo_all[b * per_block + s].astype(F32)
        lo_bf[b] = value.astype(BF16)
        lo_t[b] = value.T.astype(BF16)
        ga[dp, b * rank : (b + 1) * rank, :] = (
            adapter_scale * dot_nn(lo_bf[b], h_v[b * block : (b + 1) * block, :])
        ).astype(BF16)

    def ga_copy(k, who):
        return dp_copy(ga.at[who], ga.at[who], ga_s, ga_r, k)

    def gb_copy(k, who):
        return dp_copy(gb.at[who], gb.at[who], gb_s, gb_r, k)

    for k in range(1, nd):
        ga_copy(k, dp).start()

    siblings(1)
    step(1, False, 0, half)

    own[3].wait()
    for k in range(1, nd):
        a_copy(k, dp_from(k)).wait_recv()
    for b in range(blocks):
        a_sel[b] = a_all[tab[dp, b]]
        value = dot_nt(a_sel[b], h_v[b * block : (b + 1) * block, :])
        for i in range(rank // piece):
            li_part[b * (rank // piece) + i] = value[i * piece : (i + 1) * piece, :]
    li_rs[j] = li_part[j]

    def rs_copy(k, who, whose):
        return tp_copy(li_part.at[whose], li_rs.at[who], rs_s, rs_r, k)

    for k in range(1, ntp):
        rs_copy(k, j, tp_peer(k)).start()

    step(1, False, half)

    for k in range(1, ntp):
        rs_copy(k, tp_from(k), j).wait_recv()
    total = li_rs[0]
    for s in range(1, ntp):
        total = total + li_rs[s]
    li_all[j] = total

    def li_copy(k, who):
        return tp_copy(li_all.at[who], li_all.at[who], li_s, li_r, k)

    for k in range(1, ntp):
        li_copy(k, j).start()

    if fused:
        for d in (0, 1):
            for way in (0, 1) if d else (0,):
                @pl.when(has(way, d))
                def _():
                    fin_tiles(source(way, d))
                    hg_out(source(way, d)).start()

    siblings(2)
    step(2, fused, 0, half)

    for k in range(1, ntp):
        li_copy(k, tp_from(k)).wait_recv()
    group = rank // piece
    for b in range(blocks):
        value = jnp.concatenate([li_all[b * group + i] for i in range(group)], axis=0)
        keep = lax.broadcasted_iota(jnp.int32, (rank, block), 1) < live[dp, b]
        li_bf[b] = (value * keep.astype(F32)).astype(BF16)

    def gb_block(b):
        gb[dp, slab(b, rank), :] = (
            adapter_scale * dot_nn(li_bf[b], g_all[slab(b, block), slab(j, feat)])
        ).astype(BF16)

    def gb_blocks(d):
        for way in (0, 1) if d else (0,):
            @pl.when(has(way, d))
            def _():
                gb_block(source(way, d))

    if fused:
        for d in range(nz - 1):
            gb_blocks(d)

    def chooser(g):
        r = lax.broadcasted_iota(jnp.int32, (held * rank, blocks * rank), 0)
        q = lax.broadcasted_iota(jnp.int32, (held * rank, blocks * rank), 1)
        same = (r & (rank - 1)) == (q & (rank - 1))
        which = jnp.zeros_like(q)
        for b in range(blocks):
            lane = (q >= b * rank) & (q < (b + 1) * rank)
            which = jnp.where(lane, tab[g, b] - dp * held, which)
        hit = (r >= which * rank) & (r < (which + 1) * rank) & same
        return hit.astype(F32).astype(BF16)

    picks = [chooser(g) for g in range(nd)]
    for k in range(1, nd):
        ga_copy(k, dp_from(k)).wait_recv()
    total = dot_nn(picks[0], ga[0])
    for g in range(1, nd):
        total = total + dot_nn(picks[g], ga[g])
    oa_v[...] = total.reshape(held, rank, ff)
    oa_cp = pltpu.make_async_copy(oa_v, oa_ref, out_sem.at[0])
    oa_cp.start()
    step(2, fused, half)
    for d in range(3, nz - 1):
        siblings(d)
        step(d, fused)

    siblings(nz - 1)
    if fused:
        gb_blocks(nz - 1)
    else:
        for b in range(blocks):
            gb_block(b)
    for k in range(1, nd):
        gb_copy(k, dp).start()

    step(nz - 1, fused)
    if not fused:
        for b in range(blocks):
            fin_tiles(b)
            hg_out(b).start()

    for k in range(1, nd):
        gb_copy(k, dp_from(k)).wait_recv()
    total = dot_nn(picks[0], gb[0])
    for g in range(1, nd):
        total = total + dot_nn(picks[g], gb[g])
    ob_v[...] = total.reshape(held, rank, feat)
    ob_cp = pltpu.make_async_copy(ob_v, ob_ref, out_sem.at[1])
    ob_cp.start()

    for d in range(nz):
        for way in (0, 1):
            if d < nz - 1:
                @pl.when(has(way, d) & has(1 - way, 1))
                def _():
                    for k in range(chunks):
                        nb_copy(way, d, k).wait_send()
            if d or way == 0:
                @pl.when(has(way, d))
                def _():
                    for k in range(chunks):
                        sib_copy(way, d, k, c).wait_send()
    for k in range(1, nd):
        for copy in (b_copy, a_copy, ga_copy, gb_copy):
            copy(k, dp).wait_send()
    for k in range(1, ntp):
        bs_copy(k, j, tp_peer(k)).wait_send()
        rs_copy(k, j, tp_peer(k)).wait_send()
        lo_copy(k, j).wait_send()
        li_copy(k, j).wait_send()
    for b in range(blocks):
        hg_out(b).wait()
    oa_cp.wait()
    ob_cp.wait()


def copy_kernel(blocks, hg, oa, ob, hg_out, oa_out, ob_out, hg_v, oa_v, ob_v, in_sem, out_sem):
    size = hg.shape[0] // blocks
    stages = [
        tuple(ref.at[pl.ds(b * size, size)] for ref in (hg, hg_v, hg_out)) for b in range(blocks)
    ] + [(oa, oa_v, oa_out), (ob, ob_v, ob_out)]
    loads = [pltpu.make_async_copy(s, v, in_sem.at[i]) for i, (s, v, _) in enumerate(stages)]
    stores = [pltpu.make_async_copy(v, o, out_sem.at[i]) for i, (_, v, o) in enumerate(stages)]
    for load in loads:
        load.start()
    for load, store in zip(loads, stores):
        load.wait()
        store.start()
    for store in stores:
        store.wait()


def shards(nd, ntp, g, h, w, a, bm, tab, live):
    blocks = tab.shape[1]
    group_rows, ff = h.shape
    block = group_rows // blocks
    held, rank, _ = a.shape
    feat = bm.shape[2]
    rows, width = g.shape
    nz = ntp // 2
    chunks = max(1, min(2, rows // 16))
    tiles = ff // 256 if ff % 256 == 0 else 1
    piece = blocks * rank // ntp
    V = pltpu.VMEM
    dma = lambda *s: pltpu.SemaphoreType.DMA(s)
    scratch = [
        V((group_rows, width), BF16), V((group_rows, ff), BF16), V((ff, width), BF16),
        V((nd * held, rank, ff), BF16), V((nd * held, rank, feat), BF16),
        V((blocks, rank, ff), BF16), V((blocks, rank, feat), BF16),
        V((ntp, rank, feat), BF16), V((ntp, rank, block), BF16),
        V((blocks, rank, block), BF16), V((blocks, block, rank), BF16),
        V((ntp, piece, block), F32), V((ntp, piece, block), F32), V((ntp, piece, block), F32),
        V((blocks, rank, block), BF16),
        V((nd, blocks * rank, ff), BF16), V((nd, blocks * rank, feat), BF16),
        V((group_rows, ff), F32), V((group_rows, ff), BF16),
        V((held, rank, ff), F32), V((held, rank, feat), F32),
        dma(tiles), dma(4), dma(2 + blocks),
        dma(2, nz, chunks), dma(2, nz + 1, chunks), dma(2, nz, chunks), dma(2, nz, chunks),
        dma(nd), dma(nd), dma(nd), dma(nd), dma(ntp), dma(ntp),
        dma(ntp), dma(ntp), dma(ntp), dma(ntp), dma(ntp), dma(ntp),
        dma(nd), dma(nd), dma(nd), dma(nd),
    ]
    any_spec = pl.BlockSpec(memory_space=pl.ANY)
    smem = pl.BlockSpec(memory_space=pltpu.SMEM)
    hg, oa, ob = pl.pallas_call(
        functools.partial(
            kernel, nd, ntp, blocks, block, rank, held, rows, chunks, ff, feat, tiles
        ),
        out_shape=(
            jax.ShapeDtypeStruct((group_rows, ff), BF16),
            jax.ShapeDtypeStruct((held, rank, ff), F32),
            jax.ShapeDtypeStruct((held, rank, feat), F32),
        ),
        in_specs=[any_spec] * 5 + [smem] * 2,
        out_specs=(any_spec,) * 3,
        scratch_shapes=scratch,
        compiler_params=pltpu.CompilerParams(
            collective_id=0, has_side_effects=True, vmem_limit_bytes=62 * 1024 * 1024
        ),
    )(g, h, w, a, bm, tab, live)
    results = (hg, oa, ob)
    return pl.pallas_call(
        functools.partial(copy_kernel, blocks),
        out_shape=tuple(jax.ShapeDtypeStruct(x.shape, x.dtype) for x in results),
        in_specs=[any_spec] * 3,
        out_specs=(any_spec,) * 3,
        scratch_shapes=[V(x.shape, x.dtype) for x in results] + [dma(blocks + 2), dma(blocks + 2)],
        compiler_params=pltpu.CompilerParams(vmem_limit_bytes=62 * 1024 * 1024),
    )(*results)


def far_start(z, nz, start, size, width):
    return jnp.where(z < nz // 2, start, width - start - size)


def line_kernel(
    nd, nz, blocks, block, rank, held, rows, sizes, ff, feat, width,
    g_ref, h_ref, w_ref, a_ref, b_ref, tab, live,
    hg_v, oa_v, ob_v, g_all, w_v, acc, keep_v,
    h_v, a_own, b_own, a_out, b_out, a_in, b_from, a_sel, b_sel, b_in,
    lo_part, lo_all, lo_t, li_part, li_sib, li_sum, li_rs, li_all, ga, gb,
    w_sem, own_sem, relay,
    nb_s, nb_r, sib_s, sib_r, row_s, row_r, bdp_s, bdp_r, adp_s, adp_r,
    bs_s, bs_r, lo_s, lo_r, rs_s, rs_r, ag_s, ag_r, pair_s, pair_r,
    ga_s, ga_r, gb_s, gb_r,
):
    dp = lax.axis_index("dp")
    j = lax.axis_index("seqtp")
    z = lax.div(j, 2)
    c = lax.rem(j, 2)
    sib = z * 2 + 1 - c
    chunks = len(sizes)
    tile = 256
    tiles = ff // tile
    piece = blocks * rank // (2 * nz)
    pair_rows = 2 * block
    near = lax.div(z, 2)
    far = 1 - near
    starts = [sum(sizes[:i]) for i in range(chunks)]

    def slab(index, size):
        return pl.ds(pl.multiple_of(index * size, size), size)

    def has(way, d):
        return z >= d if way == 0 else z + d < nz

    def source(way, d):
        return z - d if way == 0 else z + d

    def dp_peer(k):
        return lax.rem(dp + k, nd)

    def dp_from(k):
        return lax.rem(dp + nd - k, nd)

    def z_peer(k):
        return lax.rem(z + k, nz)

    def z_from(k):
        return lax.rem(z + nz - k, nz)

    def toward(way):
        return (dp, j + 2 if way == 0 else j - 2)

    barrier = pltpu.get_barrier_semaphore()
    for way in (0, 1):
        @pl.when(has(1 - way, 1))
        def _():
            pl.semaphore_signal(barrier, inc=1, device_id=toward(way), device_id_type=MESH)
    pl.semaphore_signal(barrier, inc=1, device_id=(dp, sib), device_id_type=MESH)
    for k in range(1, nd):
        pl.semaphore_signal(barrier, inc=1, device_id=(dp_peer(k), j), device_id_type=MESH)

    own = [
        pltpu.make_async_copy(b_ref, b_own, own_sem.at[0]),
        pltpu.make_async_copy(g_ref, g_all.at[slab(j, rows)], own_sem.at[1]),
        pltpu.make_async_copy(h_ref, h_v, own_sem.at[2]),
        pltpu.make_async_copy(a_ref, a_own, own_sem.at[3]),
    ]
    w_cp = [
        pltpu.make_async_copy(w_ref.at[pl.ds(n * tile, tile)], w_v.at[pl.ds(n * tile, tile)], w_sem.at[n])
        for n in range(tiles)
    ]
    own[0].start()
    own[3].start()
    own[1].start()

    @pl.when(has(0, 1) & has(1, 1))
    def _():
        pl.semaphore_wait(barrier, nd + 2)

    @pl.when(jnp.logical_not(has(0, 1) & has(1, 1)))
    def _():
        pl.semaphore_wait(barrier, nd + 1)

    def part(ref, first, way, i):
        start = starts[i] if way == 1 else width - starts[i] - sizes[i]
        return ref.at[slab(first, rows), pl.ds(start, sizes[i])]

    def nb_copy(way, d, i):
        first = source(way, d) * 2 + c
        src = part(g_ref, 0, way, i) if d == 0 else part(g_all, first, way, i)
        return pltpu.make_async_remote_copy(
            src_ref=src, dst_ref=part(g_all, first, way, i),
            send_sem=nb_s.at[way, d, i], recv_sem=nb_r.at[way, d + 1, i],
            device_id=toward(way), device_id_type=MESH,
        )

    def nb_arrival(way, d, i):
        here = part(g_all, source(way, d) * 2 + c, way, i)
        return pltpu.make_async_remote_copy(
            src_ref=here, dst_ref=here,
            send_sem=nb_s.at[way, d - 1, i], recv_sem=nb_r.at[way, d, i],
            device_id=(dp, sib), device_id_type=MESH,
        )

    def sib_copy(way, d, i, core):
        here = part(g_all, source(way, d) * 2 + core, way, i)
        return pltpu.make_async_remote_copy(
            src_ref=here, dst_ref=here,
            send_sem=sib_s.at[way, d, i], recv_sem=sib_r.at[way, d, i],
            device_id=(dp, sib), device_id_type=MESH,
        )

    def row_copy(index):
        return pltpu.make_async_remote_copy(
            src_ref=g_ref, dst_ref=g_all.at[slab(index, rows)],
            send_sem=row_s, recv_sem=row_r, device_id=(dp, sib), device_id_type=MESH,
        )

    def onward(way, d):
        return has(way, d) & has(1 - way, 1)

    def advance(n):
        d, i = n // chunks, n % chunks
        if d < nz - 1:
            for way in (0, 1):
                @pl.when(onward(way, d))
                def _():
                    nb_copy(way, d, i).start()

    def event(n):
        d, i = n // chunks, n % chunks
        for way in (0, 1):
            @pl.when(has(way, d + 1))
            def _():
                nb_arrival(way, d + 1, i).wait_recv()
                sib_copy(way, d + 1, i, c).start()
        for way in (0, 1):
            @pl.when(onward(way, d))
            def _():
                nb_copy(way, d, i).wait_send()

    def landed(n):
        d, i = n // chunks + 1, n % chunks
        for way in (0, 1):
            @pl.when(has(way, d))
            def _():
                sib_copy(way, d, i, 1 - c).wait_recv()

    def dp_copy(src, dst, s, r, k):
        return pltpu.make_async_remote_copy(
            src_ref=src, dst_ref=dst, send_sem=s.at[k], recv_sem=r.at[k],
            device_id=(dp_peer(k), j), device_id_type=MESH,
        )

    def z_copy(src, dst, s, r, k):
        return pltpu.make_async_remote_copy(
            src_ref=src, dst_ref=dst, send_sem=s.at[k], recv_sem=r.at[k],
            device_id=(dp, z_peer(k) * 2 + c), device_id_type=MESH,
        )

    def core_copy(src, dst, k):
        return pltpu.make_async_remote_copy(
            src_ref=src, dst_ref=dst, send_sem=pair_s.at[k], recv_sem=pair_r.at[k],
            device_id=(dp, sib), device_id_type=MESH,
        )

    def b_copy(k, who):
        return dp_copy(b_out.at[k], b_from.at[who], bdp_s, bdp_r, k)

    def a_copy(k, who):
        return dp_copy(a_out.at[k], a_in.at[who], adp_s, adp_r, k)

    def at_owner(group, b):
        return jnp.clip(tab[group, b] - dp * held, 0, held - 1)

    def bs_copy(k, who, whose):
        return z_copy(b_sel.at[whose], b_in.at[who], bs_s, bs_r, k)

    def lo_copy(k, who):
        return z_copy(lo_all.at[who], lo_all.at[who], lo_s, lo_r, k)

    def rs_copy(k, who, whose):
        return z_copy(li_sum.at[whose], li_rs.at[who], rs_s, rs_r, k)

    def ag_copy(k, who):
        return z_copy(li_all.at[c * nz + who], li_all.at[c * nz + who], ag_s, ag_r, k)

    def ga_copy(k, who):
        return dp_copy(ga.at[who], ga.at[who], ga_s, ga_r, k)

    def gb_copy(k, who):
        return dp_copy(gb.at[who], gb.at[who], gb_s, gb_r, k)

    def lo_pair(core):
        return core_copy(lo_part.at[core], lo_part.at[core], 0)

    def li_pair(core):
        return core_copy(li_part.at[1 - core], li_sib, 1)

    def ag_pair(core):
        here = li_all.at[pl.ds(core * nz, nz)]
        return core_copy(here, here, 2)

    advance(0)
    advance(1)
    advance(2)
    row_copy(j).start()
    own[0].wait()
    for k in range(1, nd):
        for b in range(blocks):
            b_out[k, b] = b_own[at_owner(dp_peer(k), b)]
        b_copy(k, dp).start()
    for b in range(blocks):
        b_from[dp, b] = b_own[at_owner(dp, b)]
    for way in (0, 1):
        @pl.when(has(way, 1) & has(1 - way, 1))
        def _():
            pl.semaphore_signal(relay.at[way, 2], inc=1, device_id=toward(way), device_id_type=MESH)
    own[2].start()
    for n in range(tiles):
        w_cp[n].start()
    own[3].wait()
    for k in range(1, nd):
        for b in range(blocks):
            a_out[k, b] = a_own[at_owner(dp_peer(k), b)]
        a_copy(k, dp).start()
    for b in range(blocks):
        a_in[dp, b] = a_own[at_owner(dp, b)]

    for d in range(2, nz):
        for way in (0, 1):
            @pl.when(has(way, d))
            def _():
                pl.semaphore_wait(relay.at[way, d], 1)
                if d + 1 < nz:
                    @pl.when(has(1 - way, 1))
                    def _():
                        pl.semaphore_signal(
                            relay.at[way, d + 1], inc=1, device_id=toward(way), device_id_type=MESH
                        )

    for k in range(1, nd):
        b_copy(k, dp_from(k)).wait_recv()
    for b in range(blocks):
        b_sel[b] = b_from[lax.div(tab[dp, b], held), b]
    b_in[z] = b_sel[z]
    for k in range(1, nz):
        bs_copy(k, z, z_peer(k)).start()

    event(0)
    advance(3)
    event(1)
    advance(4)

    event(2)
    own[1].wait()
    row_copy(sib).wait_recv()
    for k in range(1, nz):
        bs_copy(k, z_from(k), z).wait_recv()
    low = jnp.zeros((rank, block), F32)
    for s in range(nz):
        low = low + dot_nt(b_in[s], g_all[slab(z, block), slab(2 * s + c, feat)])
    lo_part[c] = low
    lo_pair(c).start()

    lo_pair(1 - c).wait_recv()
    lanes = lax.broadcasted_iota(jnp.int32, (rank, block), 1)
    low = lo_part[0] + lo_part[1]
    lo_all[z] = (low * (lanes < live[dp, z]).astype(F32)).astype(BF16)
    for k in range(1, nz):
        lo_copy(k, z).start()
    advance(5)

    event(3)
    advance(6)
    event(4)

    for k in range(1, nd):
        a_copy(k, dp_from(k)).wait_recv()
    own[2].wait()
    for b in range(blocks):
        a_sel[b] = a_in[lax.div(tab[dp, b], held), b]
        value = dot_nt(a_sel[b], h_v[b * block : (b + 1) * block, :])
        for i in range(rank // piece):
            at = b * (rank // piece) + i
            li_part[at // nz, at % nz] = value[i * piece : (i + 1) * piece, :]
    li_pair(c).start()
    li_pair(1 - c).wait_recv()
    li_sum[...] = li_part[c] + li_sib[...]
    li_rs[z] = li_sum[z]
    for k in range(1, nz):
        rs_copy(k, z, z_peer(k)).start()
    advance(7)
    for k in range(1, nz):
        lo_copy(k, z_from(k)).wait_recv()
    for b in range(blocks):
        lo_t[b] = lo_all[b].astype(F32).T.astype(BF16)
        ga[dp, b * rank : (b + 1) * rank, :] = (
            adapter_scale * dot_nn(lo_all[b], h_v[b * block : (b + 1) * block, :])
        ).astype(BF16)
    for k in range(1, nd):
        ga_copy(k, dp).start()

    def keep_of(b):
        return (lax.broadcasted_iota(jnp.int32, (block, 1), 0) < live[dp, b]).astype(F32)

    for n in range(chunks):
        landed(n)
    for n in range(tiles):
        w_cp[n].wait()

    def near_tiles(lo, hi):
        def one(n, carry):
            cols = slab(n, tile)
            value = dot_nt(g_all[slab(near, pair_rows), :], w_v[slab(n, tile), :])
            for s in range(2):
                b = near * 2 + s
                extra = dot_nn(lo_t[b], a_sel[b, :, cols])
                total = value[s * block : (s + 1) * block] + adapter_scale * extra
                hg_v[s * block : (s + 1) * block, cols] = (total * keep_of(b)).astype(BF16)
            return carry
        lax.fori_loop(lo, hi, one, 0)

    near_tiles(0, 1)
    event(5)
    advance(8)
    near_tiles(1, 3)
    event(6)
    near_tiles(3, 4)

    for k in range(1, nz):
        rs_copy(k, z_from(k), z).wait_recv()
    total = li_rs[0]
    for s in range(1, nz):
        total = total + li_rs[s]
    whole = c * nz + z
    lanes = lax.broadcasted_iota(jnp.int32, (piece, block), 1)
    filled = live[dp, lax.div(whole * piece, rank)]
    li_all[whole] = (total * (lanes < filled).astype(F32)).astype(BF16)
    for k in range(1, nz):
        ag_copy(k, z).start()
    advance(9)
    advance(10)

    near_tiles(4, 5)
    event(7)
    advance(11)
    near_tiles(5, tiles)

    def gb_block(b):
        group = rank // piece
        rows_of = jnp.concatenate(
            [li_all[b * group + i].astype(F32) for i in range(group)], axis=0
        ).astype(BF16)
        gb[dp, slab(b, rank), :] = (
            adapter_scale * dot_nn(rows_of, g_all[slab(b, block), slab(j, feat)])
        ).astype(BF16)

    def chooser(g):
        r = lax.broadcasted_iota(jnp.int32, (held * rank, blocks * rank), 0)
        q = lax.broadcasted_iota(jnp.int32, (held * rank, blocks * rank), 1)
        same = (r & (rank - 1)) == (q & (rank - 1))
        which = jnp.zeros_like(q)
        for b in range(blocks):
            lane = (q >= b * rank) & (q < (b + 1) * rank)
            which = jnp.where(lane, tab[g, b] - dp * held, which)
        hit = (r >= which * rank) & (r < (which + 1) * rank) & same
        return hit.astype(F32).astype(BF16)

    def owned(ref):
        total = dot_nn(chooser(0), ref[0])
        for g in range(1, nd):
            total = total + dot_nn(chooser(g), ref[g])
        return total


    for s in range(2):
        b = far * 2 + s
        acc[s * block : (s + 1) * block, :] = adapter_scale * dot_nn(lo_t[b], a_sel[b])
        keep_v[s * block : (s + 1) * block, :] = jnp.broadcast_to(keep_of(b), (block, 128))

    def drain(d, stop=chunks, first=0):
        for way in (0, 1):
            for i in range(first, stop):
                if d:
                    @pl.when(has(way, d))
                    def _():
                        sib_copy(way, d, i, c).wait_send()

    row_copy(j).wait_send()
    drain(1)
    for k in range(1, nd):
        for copy in (b_copy, a_copy):
            copy(k, dp).wait_send()
    for k in range(1, nz):
        bs_copy(k, z, z_peer(k)).wait_send()
        lo_copy(k, z).wait_send()
        rs_copy(k, z, z_peer(k)).wait_send()
    for copy in (lo_pair, li_pair):
        copy(c).wait_send()
    for n in range(chunks, 2 * chunks):
        landed(n)

    def far_chunk(i):
        start = far_start(z, nz, starts[i], sizes[i], width)
        deep = pl.ds(pl.multiple_of(start, 128), sizes[i])
        for n in range(tiles):
            cols = pl.ds(n * tile, tile)
            acc[:, cols] += dot_nt(g_all[slab(far, pair_rows), deep], w_v[cols, deep])

    for i in range(chunks):
        event(2 * chunks + i)
        landed(2 * chunks + i)
        if i == 0:
            for k in range(1, nz):
                ag_copy(k, z_from(k)).wait_recv()
            ag_pair(c).start()
        if i < chunks - 1:
            far_chunk(i)
        if i == 0:
            ag_pair(1 - c).wait_recv()
            for b in range(blocks):
                gb_block(b)
            for k in range(1, nd):
                gb_copy(k, dp).start()
        if i == 1:
            for k in range(1, nd):
                ga_copy(k, dp_from(k)).wait_recv()
            oa_v[...] = owned(ga).reshape(held, rank, ff)
        if i == chunks - 2:
            for k in range(1, nd):
                gb_copy(k, dp_from(k)).wait_recv()
            ob_v[...] = owned(gb).reshape(held, rank, feat)
            for k in range(1, nd):
                gb_copy(k, dp).wait_send()
                ga_copy(k, dp).wait_send()
            for k in range(1, nz):
                ag_copy(k, z).wait_send()
            ag_pair(c).wait_send()
            drain(2)
            for d in range(3, nz):
                drain(d, chunks - 1)
    for d in range(3, nz):
        drain(d, chunks, chunks - 1)


def last_kernel(
    nz, size, hg, oa, ob, g_all, w_v, acc, keep_v, hg_out, oa_out, ob_out, far_v, sem, tile_sem
):
    z = lax.div(lax.axis_index("seqtp"), 2)
    near = lax.div(z, 2)
    pair_rows, ff = hg.shape
    width = w_v.shape[1]
    tile = 256
    near_rows = pl.ds(pl.multiple_of(near * pair_rows, pair_rows), pair_rows)
    far_rows = pl.ds(pl.multiple_of((1 - near) * pair_rows, pair_rows), pair_rows)
    copies = [(hg, hg_out.at[near_rows]), (oa, oa_out), (ob, ob_out)]
    copies = [pltpu.make_async_copy(s, o, sem.at[i]) for i, (s, o) in enumerate(copies)]
    for copy in copies:
        copy.start()
    start = far_start(z, nz, width - size, size, width)
    deep = pl.ds(pl.multiple_of(start, 128), size)
    keep = keep_v[:, :1]
    for n in range(ff // tile):
        cols = pl.ds(n * tile, tile)
        value = acc[:, cols] + dot_nt(g_all[far_rows, deep], w_v[cols, deep])
        far_v[:, cols] = (value * keep).astype(BF16)
        copies.append(
            pltpu.make_async_copy(far_v.at[:, cols], hg_out.at[far_rows, cols], tile_sem.at[n])
        )
        copies[-1].start()
    for copy in copies:
        copy.wait()


def line_shards(nd, ntp, g, h, w, a, bm, tab, live):
    blocks = tab.shape[1]
    group_rows, ff = h.shape
    block = group_rows // blocks
    held, rank, _ = a.shape
    feat = bm.shape[2]
    rows, width = g.shape
    nz = ntp // 2
    sizes = (width // 4,) * 4
    tiles = ff // 256
    chunks = len(sizes)
    piece = blocks * rank // ntp
    V = pltpu.VMEM
    dma = lambda *s: pltpu.SemaphoreType.DMA(s)
    scratch = [
        V((group_rows, ff), BF16), V((held, rank, ff), BF16), V((held, rank, feat), BF16),
        V((nd, blocks, rank, ff), BF16), V((nd, blocks, rank, feat), BF16),
        V((nd, blocks, rank, ff), BF16), V((nd, blocks, rank, feat), BF16),
        V((blocks, rank, ff), BF16), V((blocks, rank, feat), BF16), V((nz, rank, feat), BF16),
        V((2, rank, block), F32), V((blocks, rank, block), BF16), V((blocks, block, rank), BF16),
        V((2, nz, piece, block), F32), V((nz, piece, block), F32), V((nz, piece, block), F32),
        V((nz, piece, block), F32), V((ntp, piece, block), BF16),
        V((nd, blocks * rank, ff), BF16), V((nd, blocks * rank, feat), BF16),
        dma(tiles), dma(4), pltpu.SemaphoreType.REGULAR((2, nz)),
        dma(2, nz, chunks), dma(2, nz + 1, chunks), dma(2, nz, chunks), dma(2, nz, chunks),
        pltpu.SemaphoreType.DMA, pltpu.SemaphoreType.DMA,
        dma(nd), dma(nd), dma(nd), dma(nd),
        dma(nz), dma(nz), dma(nz), dma(nz), dma(nz), dma(nz), dma(nz), dma(nz), dma(3), dma(3),
        dma(nd), dma(nd), dma(nd), dma(nd),
    ]
    hbm = pl.BlockSpec(memory_space=pltpu.HBM)
    smem = pl.BlockSpec(memory_space=pltpu.SMEM)
    vmem = pl.BlockSpec(memory_space=pltpu.VMEM)
    results = pl.pallas_call(
        functools.partial(
            line_kernel, nd, nz, blocks, block, rank, held, rows, sizes, ff, feat, width
        ),
        out_shape=(
            V((2 * block, ff), BF16), V((held, rank, ff), F32), V((held, rank, feat), F32),
            V((group_rows, width), BF16), V((ff, width), BF16), V((2 * block, ff), F32),
            V((2 * block, 128), F32),
        ),
        in_specs=[hbm] * 5 + [smem] * 2,
        out_specs=(vmem,) * 7,
        scratch_shapes=scratch,
        compiler_params=pltpu.CompilerParams(
            collective_id=1, has_side_effects=True, vmem_limit_bytes=41 * 1024 * 1024
        ),
    )(g, h, w, a, bm, tab, live)
    return pl.pallas_call(
        functools.partial(last_kernel, nz, sizes[-1]),
        out_shape=(
            jax.ShapeDtypeStruct((group_rows, ff), BF16),
            jax.ShapeDtypeStruct((held, rank, ff), F32),
            jax.ShapeDtypeStruct((held, rank, feat), F32),
        ),
        in_specs=[vmem] * 7,
        out_specs=(hbm,) * 3,
        scratch_shapes=[V((2 * block, ff), BF16), dma(3), dma(tiles)],
        compiler_params=pltpu.CompilerParams(vmem_limit_bytes=8 * 1024 * 1024),
    )(*results)


def body(nd, ntp, g, h, w, a, bm, tab, live):
    blocks = tab.shape[1]
    group_rows, ff = h.shape
    rows, width = g.shape
    line = (
        ntp == 8 and blocks == 4 and 8 * rows == group_rows and ff % 256 == 0
        and width == ntp * bm.shape[2] and bm.shape[2] % 128 == 0
        and blocks * a.shape[1] == 8 * ntp
    )
    return (line_shards if line else shards)(nd, ntp, g, h, w, a, bm, tab, live)


def solution(mesh):
    in_specs = (
        P(("dp", "seqtp"), None),
        P("dp", "seqtp"),
        P("seqtp", None),
        P("dp", None, "seqtp"),
        P("dp", None, "seqtp"),
        P(),
        P(),
    )
    out_specs = (P("dp", "seqtp"), P("dp", None, "seqtp"), P("dp", None, "seqtp"))
    step = functools.partial(body, mesh.shape["dp"], mesh.shape["seqtp"])
    return jax.shard_map(step, mesh=mesh, in_specs=in_specs, out_specs=out_specs, check_vma=False)
```
